256 devices in a mesh: seq: 32 (over z, y), head: 8 (over x, core).
Axes of the slice: x: 4, y: 4, z: 8, core: 2. Of those that a mesh axis runs over, the one named last changes fastest.
Arguments:
- queries: bfloat16 [16384, 2048], P('seq', 'head'), may hold values from -6 to 6
- key_vectors: bfloat16 [16384, 2048], P('seq', 'head'), may hold values from -6 to 6
- values: bfloat16 [16384, 4096], P('seq', 'head'), may hold values from -24 to 24
- gate_log: float32 [32, 16384], P('head', 'seq'), may hold values from -1 to 0
- write_rate: float32 [32, 16384], P('head', 'seq'), as said below
- prompt_stretches: int32 [4], replicated, may hold values from 1 to 128, as said below
- decode_owner: int32 [4], replicated, may hold values from 0 to 31, as said below
- norm_gain: float32 [128], replicated, may hold values from 0.25 to 1.75
- out_weight: bfloat16 [4096, 2048], P('head'), may hold values from -0.09375 to 0.09375
Outputs:
- mixed: bfloat16 [16384, 2048], P('seq', 'head')
- decode_states: float32 [32, 32, 128, 128], P('seq', 'head')
The draws below stay inside these ranges and needn't reach their ends.
Inputs may be any that keep to these rules, and one draw needn't show every extreme that they name: `prompt_stretches`: prompts lie in order along the token dimension, each a whole number of stretches of 64 tokens; the lengths sum to 256 and the longest is exactly 128. `decode_owner`: the 4 entries are distinct. `write_rate`: every entry is positive.
All inputs are finite; a program needn't handle non-finite values.
Results may differ from the reference program's by a relative error of at most 0.014.
Values may be sent and summed in bfloat16 or wider, within the bound.
No kernel may reach another device: no remote copies, remote signals or barrier semaphores. Data moves between devices by JAX's collectives and lax.ppermute only.
A program may use at most 64 MiB of HBM per device.

```python
import math
import jax
import jax.numpy as jnp
from jax import lax

D_MODEL = 2048
HK = 16
VALUE_HEADS = 32
DK = 128
DV = 128
STRETCH = 64
PROMPTS = 4
PACKED_TOKENS = 16384
NCHUNKS = 256
LONGEST = 128
N_SEQ = 32
N_HEAD = 8


def slow_heads(key):
    share = 0.5
    return jax.random.uniform(jax.random.fold_in(key, 7), (VALUE_HEADS, 1), jnp.float32) < share


def draw_key_vectors(key, part):
    prompt_flows = jax.random.split(jax.random.fold_in(key, 31), 2)
    shared = jax.random.normal(prompt_flows[0], (NCHUNKS, 1, HK * DK), jnp.float32)
    noise = jax.random.normal(prompt_flows[1], (NCHUNKS, STRETCH, HK * DK), jnp.float32)
    combined = (3.0 * shared + noise) * 10.0 ** (-0.5)
    return jnp.clip(combined, -6.0, 6.0).reshape(PACKED_TOKENS, HK * DK).astype(jnp.bfloat16)


def draw_gate_log(key, part):
    prompt_flows = jax.random.split(jax.random.fold_in(key, 11), 5)
    interval_span = float(LONGEST * STRETCH)
    slow = slow_heads(key)
    slow_rate = jnp.exp(jax.random.uniform(prompt_flows[0], (VALUE_HEADS, 1), jnp.float32, math.log(0.05), math.log(0.3))) / interval_span
    fast_rate = jnp.exp(jax.random.uniform(prompt_flows[1], (VALUE_HEADS, 1), jnp.float32, math.log(0.0015), math.log(0.03)))
    head_write_speed = jnp.where(slow, slow_rate, fast_rate)
    random_wobble = jnp.exp(jax.random.uniform(prompt_flows[2], (VALUE_HEADS, PACKED_TOKENS), jnp.float32, math.log(0.5), math.log(2.0)))
    sudden_spike = jax.random.uniform(prompt_flows[3], (1, PACKED_TOKENS), jnp.float32) < 2.0 / interval_span
    spike_depth = jnp.log(jax.random.uniform(prompt_flows[4], (VALUE_HEADS, PACKED_TOKENS), jnp.float32, 0.5, 0.8))
    return -head_write_speed * random_wobble + jnp.where(sudden_spike, spike_depth, 0.0)


def draw_write_rate(key, part):
    prompt_flows = jax.random.split(jax.random.fold_in(key, 13), 2)
    slow = slow_heads(key)
    gentle = jax.random.uniform(prompt_flows[0], (VALUE_HEADS, PACKED_TOKENS), jnp.float32, 0.015, 0.045)
    strong = jax.random.uniform(prompt_flows[1], (VALUE_HEADS, PACKED_TOKENS), jnp.float32, 0.05, 0.95)
    return jnp.where(slow, gentle, strong)


def prompt_plan(key):
    prompt_flows = jax.random.split(jax.random.fold_in(key, 23), 3)
    others_total = NCHUNKS - LONGEST
    cuts = jax.random.permutation(prompt_flows[0], others_total - 1)[:PROMPTS - 2].astype(jnp.int32) + 1
    cuts = jnp.sort(cuts)
    bounds = jnp.concatenate([jnp.zeros((1,), jnp.int32), cuts, jnp.full((1,), others_total, jnp.int32)])
    others = bounds[1:] - bounds[:-1]
    longest_at = jax.random.randint(prompt_flows[1], (), 0, PROMPTS).astype(jnp.int32)
    index = jnp.arange(PROMPTS, dtype=jnp.int32)
    source = jnp.clip(jnp.where(index > longest_at, index - 1, index), 0, PROMPTS - 2)
    lengths = jnp.where(index == longest_at, LONGEST, others[source]).astype(jnp.int32)
    finish = jnp.cumsum(lengths).astype(jnp.int32)
    per_device = NCHUNKS // N_SEQ
    closer = (finish - 1) // per_device
    last_owner = jnp.remainder(closer[PROMPTS - 1] - 1, N_SEQ).astype(jnp.int32)
    partner = jnp.where(longest_at == PROMPTS - 1, PROMPTS - 2, longest_at).astype(jnp.int32)
    partner_owner = jnp.remainder(closer[partner] - N_SEQ // 2, N_SEQ).astype(jnp.int32)
    order = jax.random.permutation(prompt_flows[2], N_SEQ).astype(jnp.int32)
    spare = (order != last_owner) & (order != partner_owner)
    ranked = order[jnp.argsort(1 - spare.astype(jnp.int32), stable=True)]
    free_slot = (index != PROMPTS - 1) & (index != partner)
    rank = jnp.clip(jnp.cumsum(free_slot.astype(jnp.int32)) - 1, 0, N_SEQ - 1)
    owners = jnp.where(index == PROMPTS - 1, last_owner, jnp.where(index == partner, partner_owner, ranked[rank]))
    return (lengths, owners.astype(jnp.int32))


def draw_prompt_stretches(key, part):
    return prompt_plan(key)[0]


def draw_decode_owner(key, part):
    return prompt_plan(key)[1]


def block_scale(own_key, dims, shards, smallest, high):
    def one(dim, shards_of):
        heights = jax.random.uniform(jax.random.fold_in(jax.random.fold_in(own_key, 6), dim), (shards_of,), jnp.float32, smallest / len(shards), high / len(shards))
        return jnp.repeat(jnp.exp(heights), dims[dim] // shards_of).reshape((-1,) + (1,) * (len(dims) - dim - 1))

    gain = one(*shards[0])
    for cut in shards[1:]:
        gain = gain * one(*cut)
    return gain


def bell_draw(rng, dims, scale, limit, cuts=(), held_as=jnp.bfloat16):
    array = jax.random.normal(rng, dims, jnp.float32) * scale
    if len(cuts) > 0:
        array = block_scale(rng, dims, cuts, -0.22, 0.18) * array
    return jnp.clip(array, min=-limit, max=limit).astype(held_as)


def setup_inputs(seed: int = 0) -> dict:
    seeds = jax.random.split(jax.random.key(seed), 10)
    queries = bell_draw(seeds[0], (PACKED_TOKENS, HK * DK), 1.0, 6.0, ((0, 32), (1, 8)))
    key_vectors = draw_key_vectors(jax.random.fold_in(seeds[9], 71), 0)
    values = bell_draw(seeds[2], (PACKED_TOKENS, VALUE_HEADS * DV), 4.0, 24.0, ((0, 32), (1, 8)))
    gate_log = draw_gate_log(jax.random.fold_in(seeds[9], 71), 0)
    write_rate = draw_write_rate(jax.random.fold_in(seeds[9], 71), 0)
    prompt_stretches = draw_prompt_stretches(jax.random.fold_in(seeds[9], 71), 0)
    decode_owner = draw_decode_owner(jax.random.fold_in(seeds[9], 71), 0)
    norm_gain = jnp.clip(1.0 + 0.15 * jax.random.normal(seeds[7], (DV,), jnp.float32), 0.25, 1.75)
    out_weight = bell_draw(seeds[8], (VALUE_HEADS * DV, D_MODEL), (VALUE_HEADS * DV) ** -0.5, 0.09375, ((0, 8),))
    return dict(queries=queries, key_vectors=key_vectors, values=values, gate_log=gate_log, write_rate=write_rate, prompt_stretches=prompt_stretches, decode_owner=decode_owner, norm_gain=norm_gain, out_weight=out_weight)


HIGH = lax.Precision.HIGHEST

def unit_rows(vectors):
    return vectors * lax.rsqrt(lax.optimization_barrier(jnp.sum(vectors * vectors, axis=-1, keepdims=True)) + 1e-06)

def stretch_terms(query_part, key_part, value_part, gate_part, rate_part):
    length = gate_part.shape[-1]
    cumulative = jnp.cumsum(gate_part, axis=-1)
    row_index = lax.broadcasted_iota(jnp.int32, (length, length), 0)
    col_index = lax.broadcasted_iota(jnp.int32, (length, length), 1)
    spread = cumulative[:, :, None] - cumulative[:, None, :]
    strict = jnp.exp(jnp.where(row_index > col_index, spread, -jnp.inf))
    causal = jnp.exp(jnp.where(row_index >= col_index, spread, -jnp.inf))
    key_gram = jnp.einsum('hid,hjd->hij', key_part, key_part, precision=HIGH)
    system = jnp.eye(length, dtype=jnp.float32) + rate_part[:, :, None] * key_gram * strict
    growth = jnp.exp(cumulative)
    targets = jnp.concatenate([rate_part[:, :, None] * key_part * growth[:, :, None], rate_part[:, :, None] * value_part], axis=-1)
    solved = jax.scipy.linalg.solve_triangular(system, targets, lower=True, unit_diagonal=True)
    width = key_part.shape[-1]
    key_mix = solved[..., :width]
    fresh_base = solved[..., width:]
    scores = jnp.einsum('hid,hjd->hij', query_part, key_part, precision=HIGH) * causal
    query_decay = query_part * growth[:, :, None]
    key_decay = key_part * jnp.exp(cumulative[:, -1:] - cumulative)[:, :, None]
    retain = jnp.exp(cumulative[:, -1])
    return (key_mix, fresh_base, scores, query_decay, key_decay, retain)

def stretch_inputs(query_rows, key_rows, value_rows, gate_rows, rate_rows, repeat):
    length = query_rows.shape[0]
    query_part = unit_rows(query_rows.astype(jnp.float32).reshape(length, -1, DK)) * DK ** (-0.5)
    key_part = unit_rows(key_rows.astype(jnp.float32).reshape(length, -1, DK))
    query_part = jnp.repeat(query_part, repeat, axis=1).transpose(1, 0, 2)
    key_part = jnp.repeat(key_part, repeat, axis=1).transpose(1, 0, 2)
    value_part = value_rows.astype(jnp.float32).reshape(length, -1, DV).transpose(1, 0, 2)
    return stretch_terms(query_part, key_part, value_part, gate_rows, rate_rows)

def stretch_output(state, terms):
    key_mix, fresh_base, scores, query_decay, key_decay, retain = terms
    fresh = fresh_base - jnp.einsum('hcd,hde->hce', key_mix, state, precision=HIGH)
    output = jnp.einsum('hcd,hde->hce', query_decay, state, precision=HIGH) + jnp.einsum('hij,hje->hie', scores, fresh, precision=HIGH)
    following = retain[:, None, None] * state + jnp.einsum('hcd,hce->hde', key_decay, fresh, precision=HIGH)
    return (output, following)

def head_norm(output, norm_gain):
    scaled = output * lax.rsqrt(lax.optimization_barrier(jnp.mean(output * output, axis=-1, keepdims=True)) + 1e-06) * norm_gain
    return scaled.astype(jnp.bfloat16)

def prompt_layout(prompt_stretches, stretch_ids):
    finish = jnp.cumsum(prompt_stretches).astype(jnp.int32)
    begin = finish - prompt_stretches
    opens = jnp.any(stretch_ids[:, None] == begin[None, :], axis=1)
    closes = jnp.any(stretch_ids[:, None] + 1 == finish[None, :], axis=1)
    owner_prompt = lax.optimization_barrier(jnp.sum((finish[None, :] <= stretch_ids[:, None]).astype(jnp.int32), axis=1))
    return (finish, opens, closes, owner_prompt)

def reference(queries, key_vectors, values, gate_log, write_rate, prompt_stretches, decode_owner, norm_gain, out_weight):
    total = queries.shape[0]
    number = total // STRETCH
    repeat = VALUE_HEADS // HK
    stretch_ids = jnp.arange(number, dtype=jnp.int32)
    finish, opens, closes, owner_prompt = prompt_layout(prompt_stretches, stretch_ids)
    query_blocks = queries.reshape(number, STRETCH, -1)
    key_blocks = key_vectors.reshape(number, STRETCH, -1)
    value_blocks = values.reshape(number, STRETCH, -1)
    gate_blocks = gate_log.reshape(VALUE_HEADS, number, STRETCH).transpose(1, 0, 2)
    rate_blocks = write_rate.reshape(VALUE_HEADS, number, STRETCH).transpose(1, 0, 2)

    def advance(carry, inputs):
        state, table = carry
        query_rows, key_rows, value_rows, gate_rows, rate_rows, opening, closing, prompt = inputs
        terms = stretch_inputs(query_rows, key_rows, value_rows, gate_rows, rate_rows, repeat)
        state = jnp.where(opening, jnp.zeros_like(state), state)
        output, following = stretch_output(state, terms)
        prompt = jnp.minimum(prompt, PROMPTS - 1).astype(jnp.int32)
        current = lax.dynamic_index_in_dim(table, prompt, 0, keepdims=False)
        table = lax.dynamic_update_index_in_dim(table, jnp.where(closing, following, current), prompt, 0)
        return ((following, table), head_norm(output, norm_gain))
    start_state = jnp.zeros((VALUE_HEADS, DK, DV), jnp.float32)
    start_table = jnp.zeros((PROMPTS, VALUE_HEADS, DK, DV), jnp.float32)
    (final_state, table), normed = lax.scan(advance, (start_state, start_table), (query_blocks, key_blocks, value_blocks, gate_blocks, rate_blocks, opens, closes, owner_prompt))
    hidden = normed.transpose(0, 2, 1, 3).reshape(total, VALUE_HEADS * DV)
    group = VALUE_HEADS * DV // N_HEAD
    mixed = jnp.zeros((total, D_MODEL), jnp.float32)
    for index in range(N_HEAD):
        partial_sum = jnp.dot(hidden[:, index * group:(index + 1) * group].astype(jnp.float32), out_weight[index * group:(index + 1) * group].astype(jnp.float32), preferred_element_type=jnp.float32).astype(jnp.bfloat16)
        partial_sum = lax.optimization_barrier(partial_sum)
        mixed = mixed + partial_sum.astype(jnp.float32)
    decode_states = jnp.zeros((N_SEQ, VALUE_HEADS, DK, DV), jnp.float32).at[decode_owner].set(table)
    return (mixed.astype(jnp.bfloat16), decode_states)
```

```python
import jax
import jax.numpy as jnp
from jax import lax
from jax.experimental import pallas as pl
from jax.experimental.pallas import tpu as pltpu
from jax.sharding import PartitionSpec as P

DK = 128
DV = 128
STRETCH = 64
PAIR = 2 * STRETCH
ROWS, COLS = 4, 8
F32 = jnp.float32
BF16 = jnp.bfloat16
GROUP = 4

NN = (((1,), (0,)), ((), ()))
NT = (((1,), (1,)), ((), ()))
TN = (((0,), (0,)), ((), ()))


def dot(a, b, dims=NN):
    return lax.dot_general(a, b, dims, preferred_element_type=F32)


def halves(x):
    high = x.astype(BF16)
    return high, (x - high.astype(F32)).astype(BF16)


def thirds(x):
    high = x.astype(BF16)
    rest = x - high.astype(F32)
    middle = rest.astype(BF16)
    return high, middle, (rest - middle.astype(F32)).astype(BF16)


def dot3(a, b, dims=NN):
    (ah, al), (bh, bl) = a, b
    return dot(ah, bh, dims) + (dot(ah, bl, dims) + dot(al, bh, dims))


def dot_left(a, b, dims=NN):
    return dot(a[0], b, dims) + dot(a[1], b, dims)


def dot_right(a, b, dims=NN):
    return dot(a, b[0], dims) + dot(a, b[1], dims)


def spans(size, row, col):
    return (row // size) == (col // size)


def local_kernel(
    number,
    begin_ref,
    query_ref,
    key_ref,
    value_ref,
    gates_ref,
    out_ref,
    close_ref,
    block_ref,
    w_s,
    u_s,
    score_s,
    grow_s,
    keep_s,
    last_s,
    state_s,
):
    row = lax.broadcasted_iota(jnp.int32, (PAIR, PAIR), 0)
    col = lax.broadcasted_iota(jnp.int32, (PAIR, PAIR), 1)
    same = spans(STRETCH, row, col)
    eye = row == col
    causal = same & (row >= col)
    strict = same & (row > col)
    ones_low = jnp.where(causal, 1.0, 0.0).astype(BF16)
    ones_up = jnp.where(same & (row <= col), 1.0, 0.0).astype(BF16)
    ones_all = jnp.where(same, 1.0, 0.0).astype(BF16)
    ones_eye = jnp.where(eye, 1.0, 0.0).astype(BF16)
    left = jnp.concatenate([ones_low, ones_all, ones_eye], axis=0)

    def solve(step, n):
        rows = pl.ds(pl.multiple_of(n * STRETCH, STRETCH), STRETCH)
        gates = gates_ref[n]
        parts = thirds(gates)
        columns = dot(left, parts[0], NT) + (dot(left, parts[1], NT) + dot(left, parts[2], NT))
        lines = dot(parts[0], ones_up) + (dot(parts[1], ones_up) + dot(parts[2], ones_up))
        for c in range(2):
            unit = 2 * n + c
            lanes = slice(c * DK, (c + 1) * DK)
            keys = key_ref[rows, lanes]
            queries = query_ref[rows, lanes]
            kk = jnp.concatenate([keys, keys], axis=0)
            qq = jnp.concatenate([queries, queries], axis=0)
            vv = jnp.concatenate(
                [value_ref[rows, (2 * c + r) * DV : (2 * c + r + 1) * DV] for r in range(2)], axis=0
            )
            gram = dot(kk, kk, NT)
            cross = dot(qq, kk, NT)
            diagonal = jnp.where(eye, gram, 0.0)
            norm_col = lax.rsqrt(jnp.sum(diagonal, axis=1, keepdims=True) + 1e-06)
            norm_row = lax.rsqrt(jnp.sum(diagonal, axis=0, keepdims=True) + 1e-06)
            wide = qq.astype(F32)
            norm_query = lax.rsqrt(jnp.sum(wide * wide, axis=1, keepdims=True) + 1e-06) * DK ** (-0.5)
            sum_col = columns[:PAIR, c : c + 1]
            last_col = columns[PAIR : 2 * PAIR, c : c + 1]
            rate_col = columns[2 * PAIR :, 2 + c : 3 + c]
            sum_row = lines[c : c + 1]
            rate_row = gates[2 + c : 3 + c]
            decay = jnp.exp(jnp.where(causal, sum_col - sum_row, -1e30))
            system = jnp.where(strict, gram * (rate_col * norm_col) * norm_row * decay, 0.0)
            scores = cross * norm_query * norm_row * decay

            small = jnp.where(spans(8, row, col), system, 0.0)
            small_parts = halves(small)
            second = dot3(small_parts, small_parts)
            second_parts = halves(second)
            inverse = jnp.where(eye, 1.0, 0.0) - small
            inverse = inverse + dot3(halves(inverse), second_parts)
            fourth = dot3(second_parts, second_parts)
            inverse = inverse + dot3(halves(inverse), halves(fourth))
            for size in (16, 32, 64):
                edge = jnp.where(
                    spans(size, row, col) & ~spans(size // 2, row, col), system, 0.0
                )
                inverse_parts = halves(inverse)
                inner = dot3(halves(edge), inverse_parts)
                inverse = inverse - dot3(inverse_parts, halves(inner))

            w_s[unit] = dot_left(halves(inverse * (rate_row * jnp.exp(sum_row) * norm_row)), kk)
            u_s[unit] = dot_left(halves(inverse * rate_row), vv)
            score_s[unit] = scores
            grow_s[unit] = jnp.broadcast_to(jnp.exp(sum_col) * norm_query, (PAIR, DK))
            keep_s[unit] = jnp.broadcast_to(jnp.exp(last_col - sum_col) * norm_col, (PAIR, DK))
            last_s[unit] = jnp.broadcast_to(jnp.exp(last_col), (PAIR, DK))

    def solve_group(turn, carry):
        for i in range(GROUP):
            solve(turn, turn * GROUP + i)
        return carry

    lax.fori_loop(0, number // GROUP, solve_group, 0)

    close_ref[...] = jnp.zeros_like(close_ref)
    first = jnp.concatenate(
        [jnp.zeros((DK, DV), F32), jnp.where(eye, 1.0, 0.0)], axis=1
    )
    for h in range(4):
        state_s[h] = first

    def walk(n, carry):
        rows = pl.ds(pl.multiple_of(n * STRETCH, STRETCH), STRETCH)
        ident = begin_ref[4] * number + n
        opening = ident == begin_ref[0]
        for p in range(1, 4):
            opening = opening | (ident == begin_ref[p])
        alive = jnp.where(opening, 0.0, 1.0)
        for c in range(2):
            unit = 2 * n + c
            lanes = slice(c * DK, (c + 1) * DK)
            keys = key_ref[rows, lanes]
            queries = query_ref[rows, lanes]
            w_parts = halves(w_s[unit])
            grow = jnp.concatenate([grow_s[unit]] * 2, axis=1)
            keep = jnp.concatenate([keep_s[unit]] * 2, axis=1)
            pulled, asked, states = [], [], []
            for r in range(2):
                state = state_s[2 * c + r] * alive
                state_parts = halves(state)
                top = slice(r * STRETCH, (r + 1) * STRETCH)
                pulled.append(dot3((w_parts[0][top], w_parts[1][top]), state_parts))
                asked.append(dot_right(queries, state_parts))
                states.append(state)
            base = jnp.concatenate([u_s[unit], jnp.zeros((PAIR, DK), F32)], axis=1)
            fresh = base - jnp.concatenate(pulled, axis=0)
            output = grow * jnp.concatenate(asked, axis=0) + dot3(
                halves(score_s[unit]), halves(fresh)
            )
            kept = halves(keep * fresh)
            for r in range(2):
                h = 2 * c + r
                top = slice(r * STRETCH, (r + 1) * STRETCH)
                retain = last_s[unit, r * STRETCH : r * STRETCH + 1, :]
                retain = jnp.concatenate([retain] * 2, axis=1)
                state_s[h] = retain * states[r] + dot_right(
                    keys, (kept[0][top], kept[1][top]), TN
                )
                out_ref[h, rows, :] = output[top]

        for p in range(4):
            finish = begin_ref[p + 1] if p < 3 else begin_ref[5]

            @pl.when(ident + 1 == finish)
            def _(p=p):
                close_ref[p] = state_s[...]

        return carry

    lax.fori_loop(0, number, walk, 0)
    for h in range(4):
        block_ref[h, 0] = state_s[h, :, :DV].astype(BF16)
        block_ref[h, 1] = state_s[h, :, DV:].astype(BF16)


def tail_kernel(out_ref, arriving_ref, gain_ref, weight_ref, close_ref, partial_ref, final_ref):
    gain = gain_ref[...]
    hidden = []
    for h in range(4):
        arriving = arriving_ref[h]
        output = out_ref[h, :, :DV] + dot_left(halves(out_ref[h, :, DV:]), arriving)
        scale = lax.rsqrt(jnp.mean(output * output, axis=1, keepdims=True) + 1e-06)
        hidden.append((output * scale * gain).astype(BF16))
        for p in range(4):
            final_ref[p, h] = (
                close_ref[p, h, :, :DV] + dot_left(halves(close_ref[p, h, :, DV:]), arriving)
            ).astype(BF16)
    hidden = jnp.concatenate(hidden, axis=1)
    width = partial_ref.shape[2]
    for j in range(partial_ref.shape[0]):
        partial_ref[j] = dot(hidden, weight_ref[:, j * width : (j + 1) * width]).astype(BF16)


VMEM = pl.BlockSpec(memory_space=pltpu.VMEM)
SMEM = pl.BlockSpec(memory_space=pltpu.SMEM)


def shifted(block, distance):
    count = lax.axis_size("seq")
    return lax.ppermute(block, "seq", [(i, i + distance) for i in range(count - distance)])


def joined(later, earlier):
    return jnp.einsum("hde,hef->hdf", later, earlier, preferred_element_type=F32)


def body(
    queries,
    key_vectors,
    values,
    gate_log,
    write_rate,
    prompt_stretches,
    decode_owner,
    norm_gain,
    out_weight,
):
    local_rows = queries.shape[0]
    number = local_rows // STRETCH
    position = lax.axis_index("seq")
    finish = jnp.cumsum(prompt_stretches)
    begin = finish - prompt_stretches
    marks = jnp.concatenate([begin, position[None], finish[3:]]).astype(jnp.int32)
    gates = jnp.stack([gate_log, write_rate]).reshape(2, 2, 2, number, STRETCH)
    gates = gates.transpose(3, 0, 1, 2, 4).reshape(number, 4, PAIR)
    gates = jnp.concatenate([gates, jnp.zeros_like(gates)], axis=1)

    def kernel(*refs):
        local_kernel(number, *refs)

    units = 2 * number
    out, closing, block = pl.pallas_call(
        kernel,
        out_shape=(
            jax.ShapeDtypeStruct((4, local_rows, 2 * DV), F32),
            jax.ShapeDtypeStruct((4, 4, DK, 2 * DV), F32),
            jax.ShapeDtypeStruct((4, 2, DK, DV), BF16),
        ),
        in_specs=[SMEM] + [VMEM] * 4,
        out_specs=(VMEM,) * 3,
        scratch_shapes=[pltpu.VMEM((units, PAIR, DK), F32)] * 6
        + [pltpu.VMEM((4, DK, 2 * DV), F32)],
        name="local",
    )(marks, queries, key_vectors, values, gates)

    carried = block.transpose(1, 0, 2, 3)
    for distance in (1, 2, 4):
        other = shifted(carried, distance)
        made = joined(
            carried[1], jnp.concatenate([other[0], other[1]], axis=-1)
        )
        inside = made[..., :DV] + carried[0].astype(F32)
        carried = jnp.stack([inside, made[..., DV:]]).astype(BF16)
    near = shifted(carried, 1)
    far = shifted(carried[0], 9)
    arriving = (joined(near[1], far) + near[0].astype(F32)).astype(BF16)

    partial_sum, final = pl.pallas_call(
        tail_kernel,
        out_shape=(
            jax.ShapeDtypeStruct((8, local_rows, out_weight.shape[1] // 8), BF16),
            jax.ShapeDtypeStruct((4, 4, DK, DV), BF16),
        ),
        in_specs=[VMEM] * 5,
        out_specs=(VMEM,) * 2,
        name="tail",
    )(out, arriving, norm_gain[None, :], out_weight, closing)

    mixed = lax.psum_scatter(partial_sum, "head", scatter_dimension=0, tiled=True)
    finals = lax.psum(final, "seq")
    owned = jnp.zeros((4, DK, DV), F32)
    for p in range(4):
        owned = owned + jnp.where(decode_owner[p] == position, finals[p].astype(F32), 0.0)
    return (mixed[0], owned[None])


def solution(mesh):
    return jax.shard_map(
        body,
        mesh=mesh,
        in_specs=(
            P("seq", "head"),
            P("seq", "head"),
            P("seq", "head"),
            P("head", "seq"),
            P("head", "seq"),
            P(),
            P(),
            P(),
            P("head", None),
        ),
        out_specs=(P("seq", "head"), P("seq", "head", None, None)),
        check_vma=False,
    )
```

```python
import jax
import jax.numpy as jnp
from jax import lax
from jax.experimental import pallas as pl
from jax.experimental.pallas import tpu as pltpu
from jax.sharding import PartitionSpec as P


DK = 128
DV = 128
STRETCH = 64
PAIR = 2 * STRETCH
ROWS, COLS = 4, 8
F32 = jnp.float32
BF16 = jnp.bfloat16
GROUP = 4

NN = (((1,), (0,)), ((), ()))
NT = (((1,), (1,)), ((), ()))
TN = (((0,), (0,)), ((), ()))


def dot(a, b, dims=NN):
    return lax.dot_general(a, b, dims, preferred_element_type=F32)


def halves(x):
    high = x.astype(BF16)
    return high, (x - high.astype(F32)).astype(BF16)


def thirds(x):
    high = x.astype(BF16)
    rest = x - high.astype(F32)
    middle = rest.astype(BF16)
    return high, middle, (rest - middle.astype(F32)).astype(BF16)


def dot3(a, b):
    return dot_left(a, b[0]) + dot(a[0], b[1])


def dot_left(a, b):
    rows = a[0].shape[0]
    both = dot(jnp.concatenate(a, axis=0), b)
    return both[:rows] + both[rows:]


def spans(size, row, col):
    return (row // size) == (col // size)


def local_kernel(
    number,
    lengths_ref,
    position_ref,
    query_ref,
    key_ref,
    value_ref,
    gate_ref,
    rate_ref,
    out_ref,
    block_ref,
    close_ref,
    flag_ref,
    w_s,
    u_s,
    score_s,
    grow_s,
    keep_s,
    last_s,
    state_s,
    gates_s,
):
    for n in range(number):
        lanes = slice(n * STRETCH, (n + 1) * STRETCH)
        for kind, ref in enumerate((gate_ref, rate_ref)):
            for h in range(4):
                gates_s[n, 2 * kind + h // 2, 0:1, (h % 2) * STRETCH : (h % 2 + 1) * STRETCH] = ref[
                    h : h + 1, lanes
                ]

    row = lax.broadcasted_iota(jnp.int32, (PAIR, PAIR), 0)
    col = lax.broadcasted_iota(jnp.int32, (PAIR, PAIR), 1)
    same = spans(STRETCH, row, col)
    eye = row == col
    causal = same & (row >= col)
    strict = same & (row > col)
    ones_low = jnp.where(causal, 1.0, 0.0).astype(BF16)
    ones_up = jnp.where(same & (row <= col), 1.0, 0.0).astype(BF16)
    ones_all = jnp.where(same, 1.0, 0.0).astype(BF16)
    ones_eye = jnp.where(eye, 1.0, 0.0).astype(BF16)
    left = jnp.concatenate([ones_low, ones_all, ones_eye], axis=0)

    identity = jnp.where(eye, 1.0, 0.0)
    small_mask = strict & spans(8, row, col)
    edge_masks = [
        strict & spans(size, row, col) & ~spans(size // 2, row, col) for size in (16, 32, 64)
    ]

    def solve(turn, carry):
        count = 2 * GROUP
        units = [2 * turn * GROUP + i for i in range(count)]
        systems, keyed, valued, norms, rates = [], [], [], [], []
        for i in range(GROUP):
            n = turn * GROUP + i
            rows = pl.ds(pl.multiple_of(n * STRETCH, STRETCH), STRETCH)
            gates = jnp.concatenate([gates_s[n, j, 0:1, :] for j in range(4)] * 2, axis=0)
            parts = thirds(gates)
            columns = dot(left, parts[0], NT) + (
                dot(left, parts[1], NT) + dot(left, parts[2], NT)
            )
            sums = dot(parts[0], ones_up) + (dot(parts[1], ones_up) + dot(parts[2], ones_up))
            for c in range(2):
                unit = units[2 * i + c]
                lanes = slice(c * DK, (c + 1) * DK)
                keys = key_ref[rows, lanes]
                queries = query_ref[rows, lanes]
                kk = jnp.concatenate([keys, keys], axis=0)
                qq = jnp.concatenate([queries, queries], axis=0)
                vv = jnp.concatenate(
                    [
                        value_ref[rows, (2 * c + r) * DV : (2 * c + r + 1) * DV]
                        for r in range(2)
                    ],
                    axis=0,
                )
                products = dot(jnp.concatenate([kk, queries], axis=0), kk, NT)
                gram = products[:PAIR]
                cross = jnp.concatenate([products[PAIR:]] * 2, axis=0)
                diagonal = jnp.where(eye, gram, 0.0)
                norm_col = lax.rsqrt(jnp.sum(diagonal, axis=1, keepdims=True) + 1e-06)
                norm_row = lax.rsqrt(jnp.sum(diagonal, axis=0, keepdims=True) + 1e-06)
                wide = qq.astype(F32)
                norm_query = lax.rsqrt(
                    jnp.sum(wide * wide, axis=1, keepdims=True) + 1e-06
                ) * DK ** (-0.5)
                sum_col = columns[:PAIR, c : c + 1]
                last_col = columns[PAIR : 2 * PAIR, c : c + 1]
                rate_col = columns[2 * PAIR :, 2 + c : 3 + c]
                sum_row = sums[c : c + 1]
                decay = jnp.exp(jnp.where(causal, sum_col - sum_row, -1e30))
                scaled = norm_row * decay
                systems.append(
                    jnp.where(strict, gram * (rate_col * norm_col) * scaled, 0.0)
                )
                score_s[unit] = (cross * norm_query * scaled).astype(BF16)
                grow_s[unit] = jnp.broadcast_to(jnp.exp(sum_col) * norm_query, (PAIR, DK))
                keep_s[unit] = jnp.broadcast_to(
                    jnp.exp(last_col - sum_col) * norm_col, (PAIR, DK)
                )
                last_s[unit] = jnp.broadcast_to(jnp.exp(last_col), (PAIR, DK))
                keyed.append(kk)
                valued.append(vv)
                rates.append(gates[2 + c : 3 + c])
                norms.append(jnp.exp(sum_row) * norm_row)

        small = [jnp.where(small_mask, x, 0.0) for x in systems]
        small_parts = [halves(x) for x in small]
        second = [halves(dot3(x, x)) for x in small_parts]
        inverse = [identity - x for x in small]
        inverse = [x + dot3(halves(x), y) for x, y in zip(inverse, second)]
        fourth = [halves(dot3(x, x)) for x in second]
        inverse = [x + dot3(halves(x), y) for x, y in zip(inverse, fourth)]
        for mask in edge_masks:
            parts = [halves(x) for x in inverse]
            edges = [halves(jnp.where(mask, x, 0.0)) for x in systems]
            inner = [halves(dot3(x, y)) for x, y in zip(edges, parts)]
            inverse = [x - dot3(y, z) for x, y, z in zip(inverse, parts, inner)]
        for i in range(count):
            scaled = inverse[i] * rates[i]
            u_s[units[i]] = dot_left(halves(scaled), valued[i])
            high, low = halves(dot_left(halves(scaled * norms[i]), keyed[i]))
            w_s[units[i], 0] = high
            w_s[units[i], 1] = low
        return carry

    lax.fori_loop(0, number // GROUP, solve, 0)

    close_ref[...] = jnp.zeros_like(close_ref)
    finish, total = [], 0
    for p in range(4):
        total = total + lengths_ref[p]
        finish.append(total)
    row_first = (position_ref[0] // ROWS) * ROWS
    for y in range(ROWS):
        start = (row_first + y) * number
        for p in range(4):
            active = finish[p] > start
            if p > 0:
                active = active & (finish[p - 1] <= start)
            flag_ref[y, p] = jnp.broadcast_to(jnp.where(active, 1.0, 0.0), (1, DV))
    first = jnp.concatenate(
        [jnp.zeros((DK, DV), F32), jnp.where(eye, 1.0, 0.0)], axis=1
    )
    for h in range(4):
        state_s[h] = first

    def walk(n, carry):
        rows = pl.ds(pl.multiple_of(n * STRETCH, STRETCH), STRETCH)
        ident = position_ref[0] * number + n
        opening = ident == 0
        for p in range(3):
            opening = opening | (ident == finish[p])
        alive = jnp.where(opening, 0.0, 1.0)
        heads = [(c, r) for c in range(2) for r in range(2)]
        tops = [slice(r * STRETCH, (r + 1) * STRETCH) for r in range(2)]
        keys = [key_ref[rows, c * DK : (c + 1) * DK] for c in range(2)]
        queries = [query_ref[rows, c * DK : (c + 1) * DK] for c in range(2)]
        states, pulled, asked = [], [], []
        for c, r in heads:
            unit = 2 * n + c
            state = state_s[2 * c + r] * alive
            high, low = halves(state)
            w_high, w_low = w_s[unit, 0, tops[r], :], w_s[unit, 1, tops[r], :]
            first = dot(jnp.concatenate([w_high, w_low, queries[c]], axis=0), high)
            rest = dot(jnp.concatenate([w_high, queries[c]], axis=0), low)
            pulled.append(first[:STRETCH] + (first[STRETCH : 2 * STRETCH] + rest[:STRETCH]))
            asked.append(first[2 * STRETCH :] + rest[STRETCH:])
            states.append(state)
        fresh, kept = [], []
        for c in range(2):
            unit = 2 * n + c
            base = jnp.concatenate([u_s[unit], jnp.zeros((PAIR, DK), F32)], axis=1)
            keep = jnp.concatenate([keep_s[unit]] * 2, axis=1)
            fresh.append(base - jnp.concatenate(pulled[2 * c : 2 * c + 2], axis=0))
            kept.append(halves(keep * fresh[c]))
        for c, r in heads:
            h = 2 * c + r
            retain = last_s[2 * n + c, r * STRETCH : r * STRETCH + 1, :]
            retain = jnp.concatenate([retain] * 2, axis=1)
            doubled = jnp.concatenate([keys[c], keys[c]], axis=0)
            both = jnp.concatenate([kept[c][0][tops[r]], kept[c][1][tops[r]]], axis=0)
            state_s[h] = retain * states[h] + dot(doubled, both, TN)
        for c in range(2):
            unit = 2 * n + c
            grow = jnp.concatenate([grow_s[unit]] * 2, axis=1)
            high, low = halves(fresh[c])
            output = grow * jnp.concatenate(asked[2 * c : 2 * c + 2], axis=0) + (
                dot(score_s[unit], high) + dot(score_s[unit], low)
            )
            for r in range(2):
                out_ref[2 * c + r, rows, :] = output[tops[r]]

        for p in range(4):

            @pl.when(ident + 1 == finish[p])
            def _(p=p):
                for h in range(4):
                    close_ref[h, p] = state_s[h, :, :DV].astype(BF16)
                    close_ref[h, 4] = (
                        close_ref[h, 4].astype(F32) + state_s[h, :, DV:]
                    ).astype(BF16)

        return carry

    lax.fori_loop(0, number, walk, 0)
    for h in range(4):
        block_ref[h, 0] = state_s[h, :, :DV].astype(BF16)
        block_ref[h, 1] = state_s[h, :, DV:].astype(BF16)


def send_kernel(place_ref, out_ref, arriving_ref, gain_ref, weight_ref, hidden_ref, send_ref):
    gain = gain_ref[...]
    for h in range(4):
        output = out_ref[h, :, :DV] + dot_left(halves(out_ref[h, :, DV:]), arriving_ref[h])
        scale = lax.rsqrt(jnp.mean(output * output, axis=1, keepdims=True) + 1e-06)
        hidden_ref[:, h * DV : (h + 1) * DV] = (output * scale * gain).astype(BF16)
    width = send_ref.shape[2]
    place, core = place_ref[0] // 2, place_ref[0] % 2
    for k in range(4):
        j = ((place + k) % 4) * 2 + 1 - core
        columns = weight_ref[:, pl.ds(pl.multiple_of(j * width, width), width)]
        send_ref[k] = dot(hidden_ref[...], columns).astype(BF16)


def keep_kernel(place_ref, hidden_ref, weight_ref, other_ref, *kept_refs):
    width = other_ref.shape[2]
    place, core = place_ref[0] // 2, place_ref[0] % 2
    for k in range(4):
        j = ((place + k) % 4) * 2 + core
        columns = weight_ref[:, pl.ds(pl.multiple_of(j * width, width), width)]
        total = dot(hidden_ref[...], columns) + other_ref[k].astype(F32)
        kept_refs[k][...] = total.astype(BF16)


VMEM = pl.BlockSpec(memory_space=pltpu.VMEM)
SMEM = pl.BlockSpec(memory_space=pltpu.SMEM)


def shifted(block, distance):
    count = lax.axis_size("seq")
    return lax.ppermute(block, "seq", [(i, i + distance) for i in range(count - distance)])


def swapped(block, distance):
    count = lax.axis_size("seq")
    return lax.ppermute(block, "seq", [(i, i ^ distance) for i in range(count)])


def traded(blocks):
    count = lax.axis_size("seq")
    groups = [[first + y for y in range(ROWS)] for first in range(0, count, ROWS)]
    return lax.all_to_all(blocks, "seq", 0, 0, axis_index_groups=groups)


def chained(later, earlier):
    if later.ndim == 2:
        state, link = later[:, :DV], later[:, DV:]
    else:
        state, link = later[0], later[1]
    state = jnp.pad(state.astype(F32), ((0, 0), (0, DK)))
    return dot(link, earlier) + state


def program(
    queries,
    key_vectors,
    values,
    gate_log,
    write_rate,
    prompt_stretches,
    decode_owner,
    norm_gain,
    out_weight,
):
    local_rows = queries.shape[0]
    number = local_rows // STRETCH
    position = lax.axis_index("seq")
    place = lax.axis_index("head")
    here = position[None].astype(jnp.int32)

    def kernel(*refs):
        local_kernel(number, *refs)

    units = 2 * number
    out, block, closing, flags = pl.pallas_call(
        kernel,
        out_shape=(
            jax.ShapeDtypeStruct((4, local_rows, 2 * DV), F32),
            jax.ShapeDtypeStruct((4, 2, DK, DV), BF16),
            jax.ShapeDtypeStruct((4, 5, DK, DV), BF16),
            jax.ShapeDtypeStruct((ROWS, 4, 1, DV), F32),
        ),
        in_specs=[SMEM] * 2 + [VMEM] * 5,
        out_specs=(VMEM,) * 4,
        scratch_shapes=[
            pltpu.VMEM((units, 2, PAIR, DK), BF16),
            pltpu.VMEM((units, PAIR, DK), F32),
            pltpu.VMEM((units, PAIR, PAIR), BF16),
        ]
        + [pltpu.VMEM((units, PAIR, DK), F32)] * 3
        + [pltpu.VMEM((4, DK, 2 * DV), F32), pltpu.VMEM((number, 4, 8, PAIR), F32)],
        name="local",
    )(prompt_stretches, here, queries, key_vectors, values, gate_log, write_rate)

    blocks = traded(block)
    closings = traded(closing)
    both = jnp.concatenate([blocks[0, 0], blocks[0, 1]], axis=1).astype(F32)
    prefix = [both]
    for y in range(1, 4):
        both = chained(blocks[y], both.astype(BF16))
        prefix.append(both)
    before = shifted(both.astype(BF16), ROWS)
    window = chained(prefix.pop().astype(BF16), before).astype(BF16)
    near = shifted(window, ROWS)
    far = shifted(window[:, :DV], 3 * ROWS)
    entering = near[:, :DV].astype(F32) + dot(near[:, DV:], far)
    prefix = jnp.stack(prefix)
    moved = jnp.einsum(
        "yde,ef->ydf", prefix[:, :, DV:].astype(BF16), entering.astype(BF16), preferred_element_type=F32
    )
    starts = jnp.concatenate([entering[None], prefix[:, :, :DV] + moved]).astype(BF16)
    starts, closings = lax.optimization_barrier((starts, closings))
    arriving = traded(starts)

    row = position // ROWS
    moved = jnp.einsum("yde,yef->ydf", closings[:, 4], starts, preferred_element_type=F32)
    finals = sum(
        closings[y, :4].astype(F32) + flags[y] * moved[y][None] for y in range(ROWS)
    ).astype(BF16)

    width = out_weight.shape[1] // COLS
    there = place[None].astype(jnp.int32)
    hidden, outgoing = pl.pallas_call(
        send_kernel,
        out_shape=(
            jax.ShapeDtypeStruct((local_rows, 4 * DV), BF16),
            jax.ShapeDtypeStruct((4, local_rows, width), BF16),
        ),
        in_specs=[SMEM] + [VMEM] * 4,
        out_specs=(VMEM,) * 2,
        name="send",
    )(there, out, arriving, norm_gain[None, :], out_weight)
    incoming = lax.ppermute(outgoing, "head", [(i, i ^ 1) for i in range(COLS)])
    kept = pl.pallas_call(
        keep_kernel,
        out_shape=(jax.ShapeDtypeStruct((local_rows, width), BF16),) * 4,
        in_specs=[SMEM] + [VMEM] * 3,
        out_specs=(VMEM,) * 4,
        name="keep",
    )(there, hidden, out_weight, incoming)
    finals = finals + swapped(finals, ROWS)
    finals, *kept = lax.optimization_barrier((finals, *kept))
    moved = [
        lax.ppermute(kept[k], "head", [(i, (i + 2 * k) % COLS) for i in range(COLS)])
        for k in (1, 3, 2)
    ]
    for distance in (2 * ROWS, 4 * ROWS):
        finals = finals + swapped(finals, distance)
    owners = row * ROWS + jnp.arange(ROWS, dtype=jnp.int32)
    chosen = (decode_owner[None, :] == owners[:, None])[:, :, None, None]
    parcels = jnp.sum(jnp.where(chosen, finals[None].astype(F32), 0.0), axis=1).astype(BF16)
    owned = traded(parcels).astype(F32)
    mixed = kept[0].astype(F32)
    for part in moved:
        mixed = mixed + part.astype(F32)
    return (mixed.astype(BF16), owned[None])


def solution(mesh):
    return jax.shard_map(
        program,
        mesh=mesh,
        in_specs=(
            P("seq", "head"),
            P("seq", "head"),
            P("seq", "head"),
            P("head", "seq"),
            P("head", "seq"),
            P(),
            P(),
            P(),
            P("head", None),
        ),
        out_specs=(P("seq", "head"), P("seq", "head", None, None)),
        check_vma=False,
    )
```

```python
import jax
import jax.numpy as jnp
from jax import lax
from jax.experimental import pallas as pl
from jax.experimental.pallas import tpu as pltpu
from jax.sharding import PartitionSpec as P


DK = 128
DV = 128
STRETCH = 64
PAIR = 2 * STRETCH
ROWS, COLS = 4, 8
F32 = jnp.float32
BF16 = jnp.bfloat16
GROUP = 4

NN = (((1,), (0,)), ((), ()))
NT = (((1,), (1,)), ((), ()))
TN = (((0,), (0,)), ((), ()))


def dot(a, b, dims=NN):
    return lax.dot_general(a, b, dims, preferred_element_type=F32)


def halves(x):
    high = x.astype(BF16)
    return high, (x - high.astype(F32)).astype(BF16)


def thirds(x):
    high = x.astype(BF16)
    rest = x - high.astype(F32)
    middle = rest.astype(BF16)
    return high, middle, (rest - middle.astype(F32)).astype(BF16)


def dot3(a, b):
    return dot_left(a, b[0]) + dot(a[0], b[1])


def dot_left(a, b):
    rows = a[0].shape[0]
    both = dot(jnp.concatenate(a, axis=0), b)
    return both[:rows] + both[rows:]


def spans(size, row, col):
    return (row // size) == (col // size)


def local_kernel(
    number,
    lengths_ref,
    position_ref,
    query_ref,
    key_ref,
    value_ref,
    gate_ref,
    rate_ref,
    out_ref,
    block_ref,
    close_ref,
    flag_ref,
    w_s,
    u_s,
    score_s,
    grow_s,
    keep_s,
    last_s,
    state_s,
    gates_s,
):
    for n in range(number):
        lanes = slice(n * STRETCH, (n + 1) * STRETCH)
        for kind, ref in enumerate((gate_ref, rate_ref)):
            for h in range(4):
                gates_s[n, 2 * kind + h // 2, 0:1, (h % 2) * STRETCH : (h % 2 + 1) * STRETCH] = ref[
                    h : h + 1, lanes
                ]

    row = lax.broadcasted_iota(jnp.int32, (PAIR, PAIR), 0)
    col = lax.broadcasted_iota(jnp.int32, (PAIR, PAIR), 1)
    same = spans(STRETCH, row, col)
    eye = row == col
    causal = same & (row >= col)
    strict = same & (row > col)
    ones_low = jnp.where(causal, 1.0, 0.0).astype(BF16)
    ones_up = jnp.where(same & (row <= col), 1.0, 0.0).astype(BF16)
    ones_all = jnp.where(same, 1.0, 0.0).astype(BF16)
    ones_eye = jnp.where(eye, 1.0, 0.0).astype(BF16)
    left = jnp.concatenate([ones_low, ones_all, ones_eye], axis=0)

    identity = jnp.where(eye, 1.0, 0.0)
    small_mask = strict & spans(8, row, col)
    edge_masks = [
        strict & spans(size, row, col) & ~spans(size // 2, row, col) for size in (16, 32, 64)
    ]

    def solve(turn, carry):
        count = 2 * GROUP
        units = [2 * turn * GROUP + i for i in range(count)]
        systems, keyed, valued, norms, rates = [], [], [], [], []
        for i in range(GROUP):
            n = turn * GROUP + i
            rows = pl.ds(pl.multiple_of(n * STRETCH, STRETCH), STRETCH)
            gates = jnp.concatenate([gates_s[n, j, 0:1, :] for j in range(4)] * 2, axis=0)
            parts = thirds(gates)
            columns = dot(left, parts[0], NT) + (
                dot(left, parts[1], NT) + dot(left, parts[2], NT)
            )
            sums = dot(parts[0], ones_up) + (dot(parts[1], ones_up) + dot(parts[2], ones_up))
            for c in range(2):
                unit = units[2 * i + c]
                lanes = slice(c * DK, (c + 1) * DK)
                keys = key_ref[rows, lanes]
                queries = query_ref[rows, lanes]
                kk = jnp.concatenate([keys, keys], axis=0)
                qq = jnp.concatenate([queries, queries], axis=0)
                vv = jnp.concatenate(
                    [
                        value_ref[rows, (2 * c + r) * DV : (2 * c + r + 1) * DV]
                        for r in range(2)
                    ],
                    axis=0,
                )
                products = dot(jnp.concatenate([kk, queries], axis=0), kk, NT)
                gram = products[:PAIR]
                cross = jnp.concatenate([products[PAIR:]] * 2, axis=0)
                diagonal = jnp.where(eye, gram, 0.0)
                norm_col = lax.rsqrt(jnp.sum(diagonal, axis=1, keepdims=True) + 1e-06)
                norm_row = lax.rsqrt(jnp.sum(diagonal, axis=0, keepdims=True) + 1e-06)
                wide = qq.astype(F32)
                norm_query = lax.rsqrt(
                    jnp.sum(wide * wide, axis=1, keepdims=True) + 1e-06
                ) * DK ** (-0.5)
                sum_col = columns[:PAIR, c : c + 1]
                last_col = columns[PAIR : 2 * PAIR, c : c + 1]
                rate_col = columns[2 * PAIR :, 2 + c : 3 + c]
                sum_row = sums[c : c + 1]
                decay = jnp.exp(jnp.where(causal, sum_col - sum_row, -1e30))
                scaled = norm_row * decay
                systems.append(
                    jnp.where(strict, gram * (rate_col * norm_col) * scaled, 0.0)
                )
                score_s[unit] = (cross * norm_query * scaled).astype(BF16)
                grow_s[unit] = jnp.broadcast_to(jnp.exp(sum_col) * norm_query, (PAIR, DK))
                keep_s[unit] = jnp.broadcast_to(
                    jnp.exp(last_col - sum_col) * norm_col, (PAIR, DK)
                )
                last_s[unit] = jnp.broadcast_to(jnp.exp(last_col), (PAIR, DK))
                keyed.append(kk)
                valued.append(vv)
                rates.append(gates[2 + c : 3 + c])
                norms.append(jnp.exp(sum_row) * norm_row)

        small = [jnp.where(small_mask, x, 0.0) for x in systems]
        small_parts = [halves(x) for x in small]
        second = [halves(dot3(x, x)) for x in small_parts]
        inverse = [identity - x for x in small]
        inverse = [x + dot3(halves(x), y) for x, y in zip(inverse, second)]
        fourth = [halves(dot3(x, x)) for x in second]
        inverse = [x + dot3(halves(x), y) for x, y in zip(inverse, fourth)]
        for mask in edge_masks:
            parts = [halves(x) for x in inverse]
            edges = [halves(jnp.where(mask, x, 0.0)) for x in systems]
            inner = [halves(dot3(x, y)) for x, y in zip(edges, parts)]
            inverse = [x - dot3(y, z) for x, y, z in zip(inverse, parts, inner)]
        for i in range(count):
            scaled = inverse[i] * rates[i]
            u_s[units[i]] = dot_left(halves(scaled), valued[i])
            high, low = halves(dot_left(halves(scaled * norms[i]), keyed[i]))
            w_s[units[i], 0] = high
            w_s[units[i], 1] = low
        return carry

    lax.fori_loop(0, number // GROUP, solve, 0)

    close_ref[...] = jnp.zeros_like(close_ref)
    finish, total = [], 0
    for p in range(4):
        total = total + lengths_ref[p]
        finish.append(total)
    row_first = (position_ref[0] // ROWS) * ROWS
    for y in range(ROWS):
        start = (row_first + y) * number
        for p in range(4):
            active = finish[p] > start
            if p > 0:
                active = active & (finish[p - 1] <= start)
            flag_ref[y, p] = jnp.broadcast_to(jnp.where(active, 1.0, 0.0), (1, DV))
    first = jnp.concatenate(
        [jnp.zeros((DK, DV), F32), jnp.where(eye, 1.0, 0.0)], axis=1
    )
    for h in range(4):
        state_s[h] = first

    def walk(n, carry):
        rows = pl.ds(pl.multiple_of(n * STRETCH, STRETCH), STRETCH)
        ident = position_ref[0] * number + n
        opening = ident == 0
        for p in range(3):
            opening = opening | (ident == finish[p])
        alive = jnp.where(opening, 0.0, 1.0)
        heads = [(c, r) for c in range(2) for r in range(2)]
        tops = [slice(r * STRETCH, (r + 1) * STRETCH) for r in range(2)]
        keys = [key_ref[rows, c * DK : (c + 1) * DK] for c in range(2)]
        queries = [query_ref[rows, c * DK : (c + 1) * DK] for c in range(2)]
        states, pulled, asked = [], [], []
        for c, r in heads:
            unit = 2 * n + c
            state = state_s[2 * c + r] * alive
            high, low = halves(state)
            w_high, w_low = w_s[unit, 0, tops[r], :], w_s[unit, 1, tops[r], :]
            first = dot(jnp.concatenate([w_high, w_low, queries[c]], axis=0), high)
            rest = dot(jnp.concatenate([w_high, queries[c]], axis=0), low)
            pulled.append(first[:STRETCH] + (first[STRETCH : 2 * STRETCH] + rest[:STRETCH]))
            asked.append(first[2 * STRETCH :] + rest[STRETCH:])
            states.append(state)
        fresh, kept = [], []
        for c in range(2):
            unit = 2 * n + c
            base = jnp.concatenate([u_s[unit], jnp.zeros((PAIR, DK), F32)], axis=1)
            keep = jnp.concatenate([keep_s[unit]] * 2, axis=1)
            fresh.append(base - jnp.concatenate(pulled[2 * c : 2 * c + 2], axis=0))
            kept.append(halves(keep * fresh[c]))
        for c, r in heads:
            h = 2 * c + r
            retain = last_s[2 * n + c, r * STRETCH : r * STRETCH + 1, :]
            retain = jnp.concatenate([retain] * 2, axis=1)
            doubled = jnp.concatenate([keys[c], keys[c]], axis=0)
            both = jnp.concatenate([kept[c][0][tops[r]], kept[c][1][tops[r]]], axis=0)
            state_s[h] = retain * states[h] + dot(doubled, both, TN)
        for c in range(2):
            unit = 2 * n + c
            grow = jnp.concatenate([grow_s[unit]] * 2, axis=1)
            high, low = halves(fresh[c])
            output = grow * jnp.concatenate(asked[2 * c : 2 * c + 2], axis=0) + (
                dot(score_s[unit], high) + dot(score_s[unit], low)
            )
            for r in range(2):
                out_ref[2 * c + r, rows, :] = output[tops[r]]

        for p in range(4):

            @pl.when(ident + 1 == finish[p])
            def _(p=p):
                for h in range(4):
                    close_ref[h, p] = state_s[h, :, :DV].astype(BF16)
                    close_ref[h, 4] = (
                        close_ref[h, 4].astype(F32) + state_s[h, :, DV:]
                    ).astype(BF16)

        return carry

    lax.fori_loop(0, number, walk, 0)
    for h in range(4):
        block_ref[h, 0] = state_s[h, :, :DV].astype(BF16)
        block_ref[h, 1] = state_s[h, :, DV:].astype(BF16)


def send_kernel(place_ref, out_ref, arriving_ref, gain_ref, weight_ref, hidden_ref, send_ref):
    gain = gain_ref[...]
    for h in range(4):
        output = out_ref[h, :, :DV] + dot_left(halves(out_ref[h, :, DV:]), arriving_ref[h])
        scale = lax.rsqrt(jnp.mean(output * output, axis=1, keepdims=True) + 1e-06)
        hidden_ref[:, h * DV : (h + 1) * DV] = (output * scale * gain).astype(BF16)
    width = send_ref.shape[2]
    place, core = place_ref[0] // 2, place_ref[0] % 2
    for k in range(4):
        j = ((place + k) % 4) * 2 + 1 - core
        columns = weight_ref[:, pl.ds(pl.multiple_of(j * width, width), width)]
        send_ref[k] = dot(hidden_ref[...], columns).astype(BF16)


def keep_kernel(place_ref, hidden_ref, weight_ref, kept_ref):
    width = kept_ref.shape[2]
    place, core = place_ref[0] // 2, place_ref[0] % 2
    for k in range(4):
        j = ((place + k) % 4) * 2 + core
        columns = weight_ref[:, pl.ds(pl.multiple_of(j * width, width), width)]
        kept_ref[k] = dot(hidden_ref[...], columns).astype(BF16)


VMEM = pl.BlockSpec(memory_space=pltpu.VMEM)
SMEM = pl.BlockSpec(memory_space=pltpu.SMEM)


def shifted(block, distance):
    count = lax.axis_size("seq")
    return lax.ppermute(block, "seq", [(i, i + distance) for i in range(count - distance)])


def swapped(block, distance):
    count = lax.axis_size("seq")
    return lax.ppermute(block, "seq", [(i, i ^ distance) for i in range(count)])


def traded(blocks):
    count = lax.axis_size("seq")
    groups = [[first + y for y in range(ROWS)] for first in range(0, count, ROWS)]
    return lax.all_to_all(blocks, "seq", 0, 0, axis_index_groups=groups)


def chained(later, earlier):
    if later.ndim == 2:
        state, link = later[:, :DV], later[:, DV:]
    else:
        state, link = later[0], later[1]
    state = jnp.pad(state.astype(F32), ((0, 0), (0, DK)))
    return dot(link, earlier) + state


def program(
    queries,
    key_vectors,
    values,
    gate_log,
    write_rate,
    prompt_stretches,
    decode_owner,
    norm_gain,
    out_weight,
):
    local_rows = queries.shape[0]
    number = local_rows // STRETCH
    position = lax.axis_index("seq")
    place = lax.axis_index("head")
    here = position[None].astype(jnp.int32)

    def kernel(*refs):
        local_kernel(number, *refs)

    units = 2 * number
    out, block, closing, flags = pl.pallas_call(
        kernel,
        out_shape=(
            jax.ShapeDtypeStruct((4, local_rows, 2 * DV), F32),
            jax.ShapeDtypeStruct((4, 2, DK, DV), BF16),
            jax.ShapeDtypeStruct((4, 5, DK, DV), BF16),
            jax.ShapeDtypeStruct((ROWS, 4, 1, DV), F32),
        ),
        in_specs=[SMEM] * 2 + [VMEM] * 5,
        out_specs=(VMEM,) * 4,
        scratch_shapes=[
            pltpu.VMEM((units, 2, PAIR, DK), BF16),
            pltpu.VMEM((units, PAIR, DK), F32),
            pltpu.VMEM((units, PAIR, PAIR), BF16),
        ]
        + [pltpu.VMEM((units, PAIR, DK), F32)] * 3
        + [pltpu.VMEM((4, DK, 2 * DV), F32), pltpu.VMEM((number, 4, 8, PAIR), F32)],
        name="local",
    )(prompt_stretches, here, queries, key_vectors, values, gate_log, write_rate)

    blocks = traded(block)
    closings = traded(closing)
    both = jnp.concatenate([blocks[0, 0], blocks[0, 1]], axis=1).astype(F32)
    prefix = [both]
    for y in range(1, 4):
        both = chained(blocks[y], both.astype(BF16))
        prefix.append(both)
    total = prefix.pop().astype(BF16)
    far = shifted(total[:, :DV], 4 * ROWS)
    third = shifted(total, 3 * ROWS)
    second = shifted(total, 2 * ROWS)
    near = shifted(total, ROWS)
    entering = third[:, :DV].astype(F32) + dot(third[:, DV:], far)
    entering = second[:, :DV].astype(F32) + dot(second[:, DV:], entering.astype(BF16))
    entering = near[:, :DV].astype(F32) + dot(near[:, DV:], entering.astype(BF16))
    prefix = jnp.stack(prefix)
    moved = jnp.einsum(
        "yde,ef->ydf", prefix[:, :, DV:].astype(BF16), entering.astype(BF16), preferred_element_type=F32
    )
    starts = jnp.concatenate([entering[None], prefix[:, :, :DV] + moved]).astype(BF16)
    starts, closings = lax.optimization_barrier((starts, closings))
    arriving = traded(starts)

    row = position // ROWS
    moved = jnp.einsum("yde,yef->ydf", closings[:, 4], starts, preferred_element_type=F32)
    finals = sum(
        closings[y, :4].astype(F32) + flags[y] * moved[y][None] for y in range(ROWS)
    ).astype(BF16)

    other = swapped(finals, 4 * ROWS)
    finals = finals + other
    other = swapped(finals, 2 * ROWS)
    finals = finals + other
    other = swapped(finals, ROWS)
    owners = row * ROWS + jnp.arange(ROWS, dtype=jnp.int32)
    chosen = (decode_owner[None, :] == owners[:, None])[:, :, None, None]
    finals = finals.astype(F32) + other.astype(F32)
    parcels = jnp.sum(jnp.where(chosen, finals[None], 0.0), axis=1).astype(BF16)
    owned = traded(parcels).astype(F32)

    width = out_weight.shape[1] // COLS
    there = place[None].astype(jnp.int32)
    hidden, outgoing = pl.pallas_call(
        send_kernel,
        out_shape=(
            jax.ShapeDtypeStruct((local_rows, 4 * DV), BF16),
            jax.ShapeDtypeStruct((4, local_rows, width), BF16),
        ),
        in_specs=[SMEM] + [VMEM] * 4,
        out_specs=(VMEM,) * 2,
        name="send",
        compiler_params=pltpu.CompilerParams(vmem_limit_bytes=16 << 20),
    )(there, out, arriving, norm_gain[None, :], out_weight)
    incoming = lax.ppermute(outgoing, "head", [(i, i ^ 1) for i in range(COLS)])
    kept = pl.pallas_call(
        keep_kernel,
        out_shape=jax.ShapeDtypeStruct((4, local_rows, width), BF16),
        in_specs=[SMEM] + [VMEM] * 2,
        out_specs=VMEM,
        name="keep",
        compiler_params=pltpu.CompilerParams(vmem_limit_bytes=16 << 20),
    )(there, hidden, out_weight)
    sums = [kept[k].astype(F32) + incoming[k].astype(F32) for k in range(4)]
    mixed = sums[0]
    for k in (2, 1, 3):
        moved = lax.ppermute(
            sums[k].astype(BF16), "head", [(i, (i + 2 * k) % COLS) for i in range(COLS)]
        )
        mixed = mixed + moved.astype(F32)
    return (mixed.astype(BF16), owned[None])


def solution(mesh):
    return jax.shard_map(
        program,
        mesh=mesh,
        in_specs=(
            P("seq", "head"),
            P("seq", "head"),
            P("seq", "head"),
            P("head", "seq"),
            P("head", "seq"),
            P(),
            P(),
            P(),
            P("head", None),
        ),
        out_specs=(P("seq", "head"), P("seq", "head", None, None)),
        check_vma=False,
    )
```

```python
import jax
import jax.numpy as jnp
from jax import lax
from jax.experimental import pallas as pl
from jax.experimental.pallas import tpu as pltpu
from jax.sharding import PartitionSpec as P


DK = 128
DV = 128
STRETCH = 64
PAIR = 2 * STRETCH
ROWS, COLS = 4, 8
F32 = jnp.float32
BF16 = jnp.bfloat16
GROUP = 4

NN = (((1,), (0,)), ((), ()))
NT = (((1,), (1,)), ((), ()))
TN = (((0,), (0,)), ((), ()))


def dot(a, b, dims=NN):
    return lax.dot_general(a, b, dims, preferred_element_type=F32)


def halves(x):
    high = x.astype(BF16)
    return high, (x - high.astype(F32)).astype(BF16)


def thirds(x):
    high = x.astype(BF16)
    rest = x - high.astype(F32)
    middle = rest.astype(BF16)
    return high, middle, (rest - middle.astype(F32)).astype(BF16)


def dot3(a, b):
    return dot_left(a, b[0]) + dot(a[0], b[1])


def dot_left(a, b):
    rows = a[0].shape[0]
    both = dot(jnp.concatenate(a, axis=0), b)
    return both[:rows] + both[rows:]


def spans(size, row, col):
    return (row // size) == (col // size)


def local_kernel(
    number,
    lengths_ref,
    position_ref,
    query_ref,
    key_ref,
    value_ref,
    gate_ref,
    rate_ref,
    out_ref,
    link_ref,
    block_ref,
    close_ref,
    flag_ref,
    w_s,
    u_s,
    score_s,
    grow_s,
    keep_s,
    last_s,
    state_s,
    gates_s,
):
    for n in range(number):
        lanes = slice(n * STRETCH, (n + 1) * STRETCH)
        for kind, ref in enumerate((gate_ref, rate_ref)):
            for h in range(4):
                gates_s[n, 2 * kind + h // 2, 0:1, (h % 2) * STRETCH : (h % 2 + 1) * STRETCH] = ref[
                    h : h + 1, lanes
                ]

    row = lax.broadcasted_iota(jnp.int32, (PAIR, PAIR), 0)
    col = lax.broadcasted_iota(jnp.int32, (PAIR, PAIR), 1)
    same = spans(STRETCH, row, col)
    eye = row == col
    causal = same & (row >= col)
    strict = same & (row > col)
    ones_low = jnp.where(causal, 1.0, 0.0).astype(BF16)
    ones_up = jnp.where(same & (row <= col), 1.0, 0.0).astype(BF16)
    ones_all = jnp.where(same, 1.0, 0.0).astype(BF16)
    ones_eye = jnp.where(eye, 1.0, 0.0).astype(BF16)
    left = jnp.concatenate([ones_low, ones_all, ones_eye], axis=0)

    identity = jnp.where(eye, 1.0, 0.0)
    small_mask = strict & spans(8, row, col)
    edge_masks = [
        strict & spans(size, row, col) & ~spans(size // 2, row, col) for size in (16, 32, 64)
    ]

    def solve(turn, carry):
        count = 2 * GROUP
        units = [2 * turn * GROUP + i for i in range(count)]
        systems, keyed, valued, norms, rates = [], [], [], [], []
        for i in range(GROUP):
            n = turn * GROUP + i
            rows = pl.ds(pl.multiple_of(n * STRETCH, STRETCH), STRETCH)
            gates = jnp.concatenate([gates_s[n, j, 0:1, :] for j in range(4)] * 2, axis=0)
            parts = thirds(gates)
            columns = dot(left, parts[0], NT) + (
                dot(left, parts[1], NT) + dot(left, parts[2], NT)
            )
            sums = dot(parts[0], ones_up) + (dot(parts[1], ones_up) + dot(parts[2], ones_up))
            for c in range(2):
                unit = units[2 * i + c]
                lanes = slice(c * DK, (c + 1) * DK)
                keys = key_ref[rows, lanes]
                queries = query_ref[rows, lanes]
                kk = jnp.concatenate([keys, keys], axis=0)
                qq = jnp.concatenate([queries, queries], axis=0)
                vv = jnp.concatenate(
                    [
                        value_ref[rows, (2 * c + r) * DV : (2 * c + r + 1) * DV]
                        for r in range(2)
                    ],
                    axis=0,
                )
                products = dot(jnp.concatenate([kk, queries], axis=0), kk, NT)
                gram = products[:PAIR]
                cross = jnp.concatenate([products[PAIR:]] * 2, axis=0)
                diagonal = jnp.where(eye, gram, 0.0)
                norm_col = lax.rsqrt(jnp.sum(diagonal, axis=1, keepdims=True) + 1e-06)
                norm_row = lax.rsqrt(jnp.sum(diagonal, axis=0, keepdims=True) + 1e-06)
                wide = qq.astype(F32)
                norm_query = lax.rsqrt(
                    jnp.sum(wide * wide, axis=1, keepdims=True) + 1e-06
                ) * DK ** (-0.5)
                sum_col = columns[:PAIR, c : c + 1]
                last_col = columns[PAIR : 2 * PAIR, c : c + 1]
                rate_col = columns[2 * PAIR :, 2 + c : 3 + c]
                sum_row = sums[c : c + 1]
                decay = jnp.exp(jnp.where(causal, sum_col - sum_row, -1e30))
                scaled = norm_row * decay
                systems.append(
                    jnp.where(strict, gram * (rate_col * norm_col) * scaled, 0.0)
                )
                score_s[unit] = (cross * norm_query * scaled).astype(BF16)
                grow_s[unit] = jnp.broadcast_to(jnp.exp(sum_col) * norm_query, (PAIR, DK))
                keep_s[unit] = jnp.broadcast_to(
                    jnp.exp(last_col - sum_col) * norm_col, (PAIR, DK)
                )
                last_s[unit] = jnp.broadcast_to(jnp.exp(last_col), (PAIR, DK))
                keyed.append(kk)
                valued.append(vv)
                rates.append(gates[2 + c : 3 + c])
                norms.append(jnp.exp(sum_row) * norm_row)

        small = [jnp.where(small_mask, x, 0.0) for x in systems]
        small_parts = [halves(x) for x in small]
        second = [halves(dot3(x, x)) for x in small_parts]
        inverse = [identity - x for x in small]
        inverse = [x + dot3(halves(x), y) for x, y in zip(inverse, second)]
        fourth = [halves(dot3(x, x)) for x in second]
        inverse = [x + dot3(halves(x), y) for x, y in zip(inverse, fourth)]
        for mask in edge_masks:
            parts = [halves(x) for x in inverse]
            edges = [halves(jnp.where(mask, x, 0.0)) for x in systems]
            inner = [halves(dot3(x, y)) for x, y in zip(edges, parts)]
            inverse = [x - dot3(y, z) for x, y, z in zip(inverse, parts, inner)]
        for i in range(count):
            scaled = inverse[i] * rates[i]
            u_s[units[i]] = dot_left(halves(scaled), valued[i])
            high, low = halves(dot_left(halves(scaled * norms[i]), keyed[i]))
            w_s[units[i], 0] = high
            w_s[units[i], 1] = low
        return carry

    lax.fori_loop(0, number // GROUP, solve, 0)

    close_ref[...] = jnp.zeros_like(close_ref)
    finish, total = [], 0
    for p in range(4):
        total = total + lengths_ref[p]
        finish.append(total)
    inner = position_ref[0] % ROWS
    row_first = position_ref[0] - inner
    for y in range(ROWS):
        start = (row_first + (inner + y) % ROWS) * number
        for p in range(4):
            active = finish[p] > start
            if p > 0:
                active = active & (finish[p - 1] <= start)
            flag_ref[y, p] = jnp.broadcast_to(jnp.where(active, 1.0, 0.0), (1, DV))
    first = jnp.concatenate(
        [jnp.zeros((DK, DV), F32), jnp.where(eye, 1.0, 0.0)], axis=1
    )
    for h in range(4):
        state_s[h] = first

    def walk(n, carry):
        rows = pl.ds(pl.multiple_of(n * STRETCH, STRETCH), STRETCH)
        ident = position_ref[0] * number + n
        opening = ident == 0
        for p in range(3):
            opening = opening | (ident == finish[p])
        alive = jnp.where(opening, 0.0, 1.0)
        heads = [(c, r) for c in range(2) for r in range(2)]
        tops = [slice(r * STRETCH, (r + 1) * STRETCH) for r in range(2)]
        keys = [key_ref[rows, c * DK : (c + 1) * DK] for c in range(2)]
        queries = [query_ref[rows, c * DK : (c + 1) * DK] for c in range(2)]
        states, pulled, asked = [], [], []
        for c, r in heads:
            unit = 2 * n + c
            state = state_s[2 * c + r] * alive
            high, low = halves(state)
            w_high, w_low = w_s[unit, 0, tops[r], :], w_s[unit, 1, tops[r], :]
            first = dot(jnp.concatenate([w_high, w_low, queries[c]], axis=0), high)
            rest = dot(jnp.concatenate([w_high, queries[c]], axis=0), low)
            pulled.append(first[:STRETCH] + (first[STRETCH : 2 * STRETCH] + rest[:STRETCH]))
            asked.append(first[2 * STRETCH :] + rest[STRETCH:])
            states.append(state)
        fresh, kept = [], []
        for c in range(2):
            unit = 2 * n + c
            base = jnp.concatenate([u_s[unit], jnp.zeros((PAIR, DK), F32)], axis=1)
            keep = jnp.concatenate([keep_s[unit]] * 2, axis=1)
            fresh.append(base - jnp.concatenate(pulled[2 * c : 2 * c + 2], axis=0))
            kept.append(halves(keep * fresh[c]))
        for c, r in heads:
            h = 2 * c + r
            retain = last_s[2 * n + c, r * STRETCH : r * STRETCH + 1, :]
            retain = jnp.concatenate([retain] * 2, axis=1)
            doubled = jnp.concatenate([keys[c], keys[c]], axis=0)
            both = jnp.concatenate([kept[c][0][tops[r]], kept[c][1][tops[r]]], axis=0)
            state_s[h] = retain * states[h] + dot(doubled, both, TN)
        for c in range(2):
            unit = 2 * n + c
            grow = jnp.concatenate([grow_s[unit]] * 2, axis=1)
            high, low = halves(fresh[c])
            output = grow * jnp.concatenate(asked[2 * c : 2 * c + 2], axis=0) + (
                dot(score_s[unit], high) + dot(score_s[unit], low)
            )
            for r in range(2):
                out_ref[2 * c + r, rows, :] = output[tops[r], :DV]
                link_ref[2 * c + r, rows, :] = output[tops[r], DV:].astype(BF16)

        for p in range(4):

            @pl.when(ident + 1 == finish[p])
            def _(p=p):
                for h in range(4):
                    slot = (inner + ROWS - h) % ROWS
                    close_ref[slot, p] = state_s[h, :, :DV].astype(BF16)
                    close_ref[slot, 4] = (
                        close_ref[slot, 4].astype(F32) + state_s[h, :, DV:]
                    ).astype(BF16)

        return carry

    lax.fori_loop(0, number, walk, 0)
    for h in range(4):
        block_ref[h, 0] = state_s[h, :, :DV].astype(BF16)
        block_ref[h, 1] = state_s[h, :, DV:].astype(BF16)


def send_kernel(
    place_ref, out_ref, link_ref, arriving_ref, gain_ref, weight_ref, hidden_ref, send_ref
):
    gain = gain_ref[...]
    for h in range(4):
        output = out_ref[h] + dot(link_ref[h], arriving_ref[h])
        scale = lax.rsqrt(jnp.mean(output * output, axis=1, keepdims=True) + 1e-06)
        hidden_ref[:, h * DV : (h + 1) * DV] = (output * scale * gain).astype(BF16)
    width = send_ref.shape[2]
    place, core = place_ref[0] // 2, place_ref[0] % 2
    for k in range(4):
        j = ((place + k) % 4) * 2 + 1 - core
        columns = weight_ref[:, pl.ds(pl.multiple_of(j * width, width), width)]
        send_ref[k] = dot(hidden_ref[...], columns).astype(BF16)


def keep_kernel(place_ref, hidden_ref, weight_ref, kept_ref):
    width = kept_ref.shape[2]
    place, core = place_ref[0] // 2, place_ref[0] % 2
    for k in range(4):
        j = ((place + k) % 4) * 2 + core
        columns = weight_ref[:, pl.ds(pl.multiple_of(j * width, width), width)]
        kept_ref[k] = dot(hidden_ref[...], columns).astype(BF16)


VMEM = pl.BlockSpec(memory_space=pltpu.VMEM)
SMEM = pl.BlockSpec(memory_space=pltpu.SMEM)


def shifted(block, distance):
    count = lax.axis_size("seq")
    return lax.ppermute(block, "seq", [(i, i + distance) for i in range(count - distance)])


def swapped(block, distance):
    count = lax.axis_size("seq")
    return lax.ppermute(block, "seq", [(i, i ^ distance) for i in range(count)])


def traded(blocks):
    count = lax.axis_size("seq")
    groups = [[first + y for y in range(ROWS)] for first in range(0, count, ROWS)]
    return lax.all_to_all(blocks, "seq", 0, 0, axis_index_groups=groups)


def chained(later, earlier):
    if later.ndim == 2:
        state, link = later[:, :DV], later[:, DV:]
    else:
        state, link = later[0], later[1]
    state = jnp.pad(state.astype(F32), ((0, 0), (0, DK)))
    return dot(link, earlier) + state


def program(
    queries,
    key_vectors,
    values,
    gate_log,
    write_rate,
    prompt_stretches,
    decode_owner,
    norm_gain,
    out_weight,
):
    local_rows = queries.shape[0]
    number = local_rows // STRETCH
    position = lax.axis_index("seq")
    place = lax.axis_index("head")
    here = position[None].astype(jnp.int32)

    def kernel(*refs):
        local_kernel(number, *refs)

    units = 2 * number
    out, links, block, closing, flags = pl.pallas_call(
        kernel,
        out_shape=(
            jax.ShapeDtypeStruct((4, local_rows, DV), F32),
            jax.ShapeDtypeStruct((4, local_rows, DK), BF16),
            jax.ShapeDtypeStruct((4, 2, DK, DV), BF16),
            jax.ShapeDtypeStruct((4, 5, DK, DV), BF16),
            jax.ShapeDtypeStruct((ROWS, 4, 1, DV), F32),
        ),
        in_specs=[SMEM] * 2 + [VMEM] * 5,
        out_specs=(VMEM,) * 5,
        scratch_shapes=[
            pltpu.VMEM((units, 2, PAIR, DK), BF16),
            pltpu.VMEM((units, PAIR, DK), F32),
            pltpu.VMEM((units, PAIR, PAIR), BF16),
        ]
        + [pltpu.VMEM((units, PAIR, DK), F32)] * 3
        + [pltpu.VMEM((4, DK, 2 * DV), F32), pltpu.VMEM((number, 4, 8, PAIR), F32)],
        name="local",
    )(prompt_stretches, here, queries, key_vectors, values, gate_log, write_rate)

    blocks = traded(block)
    count = lax.axis_size("seq")
    closings = [closing[0]]
    for k in range(1, ROWS):
        route = [(i, (i // ROWS) * ROWS + (i - k) % ROWS) for i in range(count)]
        closings.append(lax.ppermute(closing[k], "seq", route))
    both = jnp.concatenate([blocks[0, 0], blocks[0, 1]], axis=1).astype(F32)
    prefix = [both]
    for y in range(1, 4):
        both = chained(blocks[y], both.astype(BF16))
        prefix.append(both)
    total = prefix.pop().astype(BF16)
    last = dot(blocks[3, 1], prefix[-1][:, :DV].astype(BF16)) + blocks[3, 0].astype(F32)
    far = shifted(last.astype(BF16), 4 * ROWS)
    third = shifted(total, 3 * ROWS)
    second = shifted(total, 2 * ROWS)
    near = shifted(total, ROWS)
    entering = third[:, :DV].astype(F32) + dot(third[:, DV:], far)
    entering = second[:, :DV].astype(F32) + dot(second[:, DV:], entering.astype(BF16))
    entering = near[:, :DV].astype(F32) + dot(near[:, DV:], entering.astype(BF16))
    prefix = jnp.stack(prefix)
    moved = jnp.einsum(
        "yde,ef->ydf", prefix[:, :, DV:].astype(BF16), entering.astype(BF16), preferred_element_type=F32
    )
    starts = jnp.concatenate([entering[None], prefix[:, :, :DV] + moved]).astype(BF16)
    arriving = traded(starts)

    row = position // ROWS
    turned = lax.dynamic_slice_in_dim(
        jnp.concatenate([starts, starts]), position % ROWS, ROWS, axis=0
    )
    finals = sum(
        closings[k][:4].astype(F32) + flags[k] * dot(closings[k][4], turned[k])[None]
        for k in range(ROWS)
    ).astype(BF16)

    other = swapped(finals, 4 * ROWS)
    finals = finals + other
    other = swapped(finals, 2 * ROWS)
    width = out_weight.shape[1] // COLS
    out_weight = pltpu.with_memory_space_constraint(out_weight, pltpu.HBM)
    there = place[None].astype(jnp.int32)
    hidden, outgoing = pl.pallas_call(
        send_kernel,
        out_shape=(
            jax.ShapeDtypeStruct((local_rows, 4 * DV), BF16),
            jax.ShapeDtypeStruct((4, local_rows, width), BF16),
        ),
        in_specs=[SMEM] + [VMEM] * 5,
        out_specs=(VMEM,) * 2,
        name="send",
        compiler_params=pltpu.CompilerParams(vmem_limit_bytes=16 << 20),
    )(there, out, links, arriving, norm_gain[None, :], out_weight)
    incoming = lax.ppermute(outgoing, "head", [(i, i ^ 1) for i in range(COLS)])
    kept = pl.pallas_call(
        keep_kernel,
        out_shape=jax.ShapeDtypeStruct((4, local_rows, width), BF16),
        in_specs=[SMEM] + [VMEM] * 2,
        out_specs=VMEM,
        name="keep",
        compiler_params=pltpu.CompilerParams(vmem_limit_bytes=16 << 20),
    )(there, hidden, out_weight)
    sums = [kept[k].astype(F32) + incoming[k].astype(F32) for k in range(4)]
    parts = [sums[k].astype(BF16) for k in range(4)]
    finals, _ = lax.optimization_barrier((finals, parts[2]))
    finals = finals + other
    other = swapped(finals, ROWS)
    owners = row * ROWS + jnp.arange(ROWS, dtype=jnp.int32)
    chosen = (decode_owner[None, :] == owners[:, None])[:, :, None, None]
    finals = finals.astype(F32) + other.astype(F32)
    parcels = jnp.sum(jnp.where(chosen, finals[None], 0.0), axis=1).astype(BF16)
    owned = traded(parcels).astype(F32)

    mixed = sums[0]
    for k in (2, 1, 3):
        moved = lax.ppermute(
            parts[k], "head", [(i, (i + 2 * k) % COLS) for i in range(COLS)]
        )
        mixed = mixed + moved.astype(F32)
    return (mixed.astype(BF16), owned[None])


def solution(mesh):
    return jax.shard_map(
        program,
        mesh=mesh,
        in_specs=(
            P("seq", "head"),
            P("seq", "head"),
            P("seq", "head"),
            P("head", "seq"),
            P("head", "seq"),
            P(),
            P(),
            P(),
            P("head", None),
        ),
        out_specs=(P("seq", "head"), P("seq", "head", None, None)),
        check_vma=False,
    )
```

```python
import jax
import jax.numpy as jnp
from jax import lax
from jax.experimental import pallas as pl
from jax.experimental.pallas import tpu as pltpu
from jax.sharding import PartitionSpec as P


DK = 128
DV = 128
STRETCH = 64
PAIR = 2 * STRETCH
ROWS, COLS = 4, 8
F32 = jnp.float32
BF16 = jnp.bfloat16
GROUP = 4

NN = (((1,), (0,)), ((), ()))
NT = (((1,), (1,)), ((), ()))
TN = (((0,), (0,)), ((), ()))


def dot(a, b, dims=NN):
    return lax.dot_general(a, b, dims, preferred_element_type=F32)


def halves(x):
    high = x.astype(BF16)
    return high, (x - high.astype(F32)).astype(BF16)


def thirds(x):
    high = x.astype(BF16)
    rest = x - high.astype(F32)
    middle = rest.astype(BF16)
    return high, middle, (rest - middle.astype(F32)).astype(BF16)


def dot3(a, b):
    return dot_left(a, b[0]) + dot(a[0], b[1])


def dot_left(a, b):
    rows = a[0].shape[0]
    both = dot(jnp.concatenate(a, axis=0), b)
    return both[:rows] + both[rows:]


def spans(size, row, col):
    return (row // size) == (col // size)


def local_kernel(
    number,
    lengths_ref,
    position_ref,
    query_ref,
    key_ref,
    value_ref,
    gate_ref,
    rate_ref,
    out_ref,
    link_ref,
    block_ref,
    close_ref,
    flag_ref,
    w_s,
    u_s,
    score_s,
    grow_s,
    keep_s,
    last_s,
    state_s,
    gates_s,
):
    for n in range(number):
        lanes = slice(n * STRETCH, (n + 1) * STRETCH)
        for kind, ref in enumerate((gate_ref, rate_ref)):
            for h in range(4):
                gates_s[n, 2 * kind + h // 2, 0:1, (h % 2) * STRETCH : (h % 2 + 1) * STRETCH] = ref[
                    h : h + 1, lanes
                ]

    row = lax.broadcasted_iota(jnp.int32, (PAIR, PAIR), 0)
    col = lax.broadcasted_iota(jnp.int32, (PAIR, PAIR), 1)
    same = spans(STRETCH, row, col)
    eye = row == col
    causal = same & (row >= col)
    strict = same & (row > col)
    ones_low = jnp.where(causal, 1.0, 0.0).astype(BF16)
    ones_up = jnp.where(same & (row <= col), 1.0, 0.0).astype(BF16)
    ones_all = jnp.where(same, 1.0, 0.0).astype(BF16)
    ones_eye = jnp.where(eye, 1.0, 0.0).astype(BF16)
    left = jnp.concatenate([ones_low, ones_all, ones_eye], axis=0)

    identity = jnp.where(eye, 1.0, 0.0)
    small_mask = strict & spans(8, row, col)
    edge_masks = [
        strict & spans(size, row, col) & ~spans(size // 2, row, col) for size in (16, 32, 64)
    ]

    def solve(turn, carry):
        count = 2 * GROUP
        units = [2 * turn * GROUP + i for i in range(count)]
        systems, keyed, valued, norms, rates = [], [], [], [], []
        for i in range(GROUP):
            n = turn * GROUP + i
            rows = pl.ds(pl.multiple_of(n * STRETCH, STRETCH), STRETCH)
            gates = jnp.concatenate([gates_s[n, j, 0:1, :] for j in range(4)] * 2, axis=0)
            parts = thirds(gates)
            columns = dot(left, parts[0], NT) + (
                dot(left, parts[1], NT) + dot(left, parts[2], NT)
            )
            sums = dot(parts[0], ones_up) + (dot(parts[1], ones_up) + dot(parts[2], ones_up))
            for c in range(2):
                unit = units[2 * i + c]
                lanes = slice(c * DK, (c + 1) * DK)
                keys = key_ref[rows, lanes]
                queries = query_ref[rows, lanes]
                kk = jnp.concatenate([keys, keys], axis=0)
                qq = jnp.concatenate([queries, queries], axis=0)
                vv = jnp.concatenate(
                    [
                        value_ref[rows, (2 * c + r) * DV : (2 * c + r + 1) * DV]
                        for r in range(2)
                    ],
                    axis=0,
                )
                products = dot(jnp.concatenate([kk, queries], axis=0), kk, NT)
                gram = products[:PAIR]
                cross = jnp.concatenate([products[PAIR:]] * 2, axis=0)
                diagonal = jnp.where(eye, gram, 0.0)
                norm_col = lax.rsqrt(jnp.sum(diagonal, axis=1, keepdims=True) + 1e-06)
                norm_row = lax.rsqrt(jnp.sum(diagonal, axis=0, keepdims=True) + 1e-06)
                wide = qq.astype(F32)
                norm_query = lax.rsqrt(
                    jnp.sum(wide * wide, axis=1, keepdims=True) + 1e-06
                ) * DK ** (-0.5)
                sum_col = columns[:PAIR, c : c + 1]
                last_col = columns[PAIR : 2 * PAIR, c : c + 1]
                rate_col = columns[2 * PAIR :, 2 + c : 3 + c]
                sum_row = sums[c : c + 1]
                decay = jnp.exp(jnp.where(causal, sum_col - sum_row, -1e30))
                scaled = norm_row * decay
                systems.append(
                    jnp.where(strict, gram * (rate_col * norm_col) * scaled, 0.0)
                )
                score_s[unit] = (cross * norm_query * scaled).astype(BF16)
                grow_s[unit] = jnp.broadcast_to(jnp.exp(sum_col) * norm_query, (PAIR, DK))
                keep_s[unit] = jnp.broadcast_to(
                    jnp.exp(last_col - sum_col) * norm_col, (PAIR, DK)
                )
                last_s[unit] = jnp.broadcast_to(jnp.exp(last_col), (PAIR, DK))
                keyed.append(kk)
                valued.append(vv)
                rates.append(gates[2 + c : 3 + c])
                norms.append(jnp.exp(sum_row) * norm_row)

        small = [jnp.where(small_mask, x, 0.0) for x in systems]
        small_parts = [halves(x) for x in small]
        second = [halves(dot3(x, x)) for x in small_parts]
        inverse = [identity - x for x in small]
        inverse = [x + dot3(halves(x), y) for x, y in zip(inverse, second)]
        fourth = [halves(dot3(x, x)) for x in second]
        inverse = [x + dot3(halves(x), y) for x, y in zip(inverse, fourth)]
        for mask in edge_masks:
            parts = [halves(x) for x in inverse]
            edges = [halves(jnp.where(mask, x, 0.0)) for x in systems]
            inner = [halves(dot3(x, y)) for x, y in zip(edges, parts)]
            inverse = [x - dot3(y, z) for x, y, z in zip(inverse, parts, inner)]
        for i in range(count):
            scaled = inverse[i] * rates[i]
            u_s[units[i]] = dot_left(halves(scaled), valued[i])
            high, low = halves(dot_left(halves(scaled * norms[i]), keyed[i]))
            w_s[units[i], 0] = high
            w_s[units[i], 1] = low
        return carry

    lax.fori_loop(0, number // GROUP, solve, 0)

    close_ref[...] = jnp.zeros_like(close_ref)
    finish, total = [], 0
    for p in range(4):
        total = total + lengths_ref[p]
        finish.append(total)
    inner = position_ref[0] % ROWS
    row_first = position_ref[0] - inner
    for y in range(ROWS):
        start = (row_first + (inner + y) % ROWS) * number
        for p in range(4):
            active = finish[p] > start
            if p > 0:
                active = active & (finish[p - 1] <= start)
            flag_ref[y, p] = jnp.broadcast_to(jnp.where(active, 1.0, 0.0), (1, DV))
    first = jnp.concatenate(
        [jnp.zeros((DK, DV), F32), jnp.where(eye, 1.0, 0.0)], axis=1
    )
    for h in range(4):
        state_s[h] = first

    def walk(n, carry):
        rows = pl.ds(pl.multiple_of(n * STRETCH, STRETCH), STRETCH)
        ident = position_ref[0] * number + n
        opening = ident == 0
        for p in range(3):
            opening = opening | (ident == finish[p])
        alive = jnp.where(opening, 0.0, 1.0)
        heads = [(c, r) for c in range(2) for r in range(2)]
        tops = [slice(r * STRETCH, (r + 1) * STRETCH) for r in range(2)]
        keys = [key_ref[rows, c * DK : (c + 1) * DK] for c in range(2)]
        queries = [query_ref[rows, c * DK : (c + 1) * DK] for c in range(2)]
        states, pulled, asked = [], [], []
        for c, r in heads:
            unit = 2 * n + c
            state = state_s[2 * c + r] * alive
            high, low = halves(state)
            w_high, w_low = w_s[unit, 0, tops[r], :], w_s[unit, 1, tops[r], :]
            first = dot(jnp.concatenate([w_high, w_low, queries[c]], axis=0), high)
            rest = dot(jnp.concatenate([w_high, queries[c]], axis=0), low)
            pulled.append(first[:STRETCH] + (first[STRETCH : 2 * STRETCH] + rest[:STRETCH]))
            asked.append(first[2 * STRETCH :] + rest[STRETCH:])
            states.append(state)
        fresh, kept = [], []
        for c in range(2):
            unit = 2 * n + c
            base = jnp.concatenate([u_s[unit], jnp.zeros((PAIR, DK), F32)], axis=1)
            keep = jnp.concatenate([keep_s[unit]] * 2, axis=1)
            fresh.append(base - jnp.concatenate(pulled[2 * c : 2 * c + 2], axis=0))
            kept.append(halves(keep * fresh[c]))
        for c, r in heads:
            h = 2 * c + r
            retain = last_s[2 * n + c, r * STRETCH : r * STRETCH + 1, :]
            retain = jnp.concatenate([retain] * 2, axis=1)
            doubled = jnp.concatenate([keys[c], keys[c]], axis=0)
            both = jnp.concatenate([kept[c][0][tops[r]], kept[c][1][tops[r]]], axis=0)
            state_s[h] = retain * states[h] + dot(doubled, both, TN)
        for c in range(2):
            unit = 2 * n + c
            grow = jnp.concatenate([grow_s[unit]] * 2, axis=1)
            high, low = halves(fresh[c])
            output = grow * jnp.concatenate(asked[2 * c : 2 * c + 2], axis=0) + (
                dot(score_s[unit], high) + dot(score_s[unit], low)
            )
            for r in range(2):
                out_ref[2 * c + r, rows, :] = output[tops[r], :DV]
                link_ref[2 * c + r, rows, :] = output[tops[r], DV:].astype(BF16)

        for p in range(4):

            @pl.when(ident + 1 == finish[p])
            def _(p=p):
                for h in range(4):
                    slot = (inner + ROWS - h) % ROWS
                    close_ref[slot, p] = state_s[h, :, :DV].astype(BF16)
                    close_ref[slot, 4] = (
                        close_ref[slot, 4].astype(F32) + state_s[h, :, DV:]
                    ).astype(BF16)

        return carry

    lax.fori_loop(0, number, walk, 0)
    for h in range(4):
        block_ref[h, 0] = state_s[h, :, :DV].astype(BF16)
        block_ref[h, 1] = state_s[h, :, DV:].astype(BF16)


def send_kernel(
    place_ref, out_ref, link_ref, arriving_ref, gain_ref, weight_ref, hidden_ref, send_ref
):
    gain = gain_ref[...]
    for h in range(4):
        output = out_ref[h] + dot(link_ref[h], arriving_ref[h])
        scale = lax.rsqrt(jnp.mean(output * output, axis=1, keepdims=True) + 1e-06)
        hidden_ref[:, h * DV : (h + 1) * DV] = (output * scale * gain).astype(BF16)
    width = send_ref.shape[2]
    place, core = place_ref[0] // 2, place_ref[0] % 2
    for k in range(4):
        j = ((place + k) % 4) * 2 + 1 - core
        columns = weight_ref[:, pl.ds(pl.multiple_of(j * width, width), width)]
        send_ref[k] = dot(hidden_ref[...], columns).astype(BF16)


def keep_kernel(place_ref, hidden_ref, weight_ref, kept_ref):
    width = kept_ref.shape[2]
    place, core = place_ref[0] // 2, place_ref[0] % 2
    for k in range(4):
        j = ((place + k) % 4) * 2 + core
        columns = weight_ref[:, pl.ds(pl.multiple_of(j * width, width), width)]
        kept_ref[k] = dot(hidden_ref[...], columns).astype(BF16)


VMEM = pl.BlockSpec(memory_space=pltpu.VMEM)
SMEM = pl.BlockSpec(memory_space=pltpu.SMEM)


def shifted(block, distance):
    count = lax.axis_size("seq")
    return lax.ppermute(block, "seq", [(i, i + distance) for i in range(count - distance)])


def swapped(block, distance):
    count = lax.axis_size("seq")
    return lax.ppermute(block, "seq", [(i, i ^ distance) for i in range(count)])


def traded(blocks):
    count = lax.axis_size("seq")
    groups = [[first + y for y in range(ROWS)] for first in range(0, count, ROWS)]
    return lax.all_to_all(blocks, "seq", 0, 0, axis_index_groups=groups)


def chained(later, earlier):
    if later.ndim == 2:
        state, link = later[:, :DV], later[:, DV:]
    else:
        state, link = later[0], later[1]
    state = jnp.pad(state.astype(F32), ((0, 0), (0, DK)))
    return dot(link, earlier) + state


def program(
    queries,
    key_vectors,
    values,
    gate_log,
    write_rate,
    prompt_stretches,
    decode_owner,
    norm_gain,
    out_weight,
):
    local_rows = queries.shape[0]
    number = local_rows // STRETCH
    position = lax.axis_index("seq")
    place = lax.axis_index("head")
    here = position[None].astype(jnp.int32)

    def kernel(*refs):
        local_kernel(number, *refs)

    units = 2 * number
    out, links, block, closing, flags = pl.pallas_call(
        kernel,
        out_shape=(
            jax.ShapeDtypeStruct((4, local_rows, DV), F32),
            jax.ShapeDtypeStruct((4, local_rows, DK), BF16),
            jax.ShapeDtypeStruct((4, 2, DK, DV), BF16),
            jax.ShapeDtypeStruct((4, 5, DK, DV), BF16),
            jax.ShapeDtypeStruct((ROWS, 4, 1, DV), F32),
        ),
        in_specs=[SMEM] * 2 + [VMEM] * 5,
        out_specs=(VMEM,) * 5,
        scratch_shapes=[
            pltpu.VMEM((units, 2, PAIR, DK), BF16),
            pltpu.VMEM((units, PAIR, DK), F32),
            pltpu.VMEM((units, PAIR, PAIR), BF16),
        ]
        + [pltpu.VMEM((units, PAIR, DK), F32)] * 3
        + [pltpu.VMEM((4, DK, 2 * DV), F32), pltpu.VMEM((number, 4, 8, PAIR), F32)],
        name="local",
    )(prompt_stretches, here, queries, key_vectors, values, gate_log, write_rate)

    blocks = traded(block)
    count = lax.axis_size("seq")
    closings = [closing[0]]
    for k in range(1, ROWS):
        route = [(i, (i // ROWS) * ROWS + (i - k) % ROWS) for i in range(count)]
        closings.append(lax.ppermute(closing[k], "seq", route))
    both = jnp.concatenate([blocks[0, 0], blocks[0, 1]], axis=1).astype(F32)
    prefix = [both]
    for y in range(1, 4):
        both = chained(blocks[y], both.astype(BF16))
        prefix.append(both)
    total = prefix.pop().astype(BF16)
    last = dot(blocks[3, 1], prefix[-1][:, :DV].astype(BF16)) + blocks[3, 0].astype(F32)
    far = shifted(last.astype(BF16), 4 * ROWS)
    third = shifted(total, 3 * ROWS)
    second = shifted(total, 2 * ROWS)
    near = shifted(total, ROWS)
    entering = third[:, :DV].astype(F32) + dot(third[:, DV:], far)
    entering = second[:, :DV].astype(F32) + dot(second[:, DV:], entering.astype(BF16))
    entering = near[:, :DV].astype(F32) + dot(near[:, DV:], entering.astype(BF16))
    prefix = jnp.stack(prefix)
    moved = jnp.einsum(
        "yde,ef->ydf", prefix[:, :, DV:].astype(BF16), entering.astype(BF16), preferred_element_type=F32
    )
    starts = jnp.concatenate([entering[None], prefix[:, :, :DV] + moved]).astype(BF16)
    arriving = traded(starts)

    row = position // ROWS
    turned = lax.dynamic_slice_in_dim(
        jnp.concatenate([starts, starts]), position % ROWS, ROWS, axis=0
    )
    carried = [dot(closings[k][4], turned[k])[None] for k in range(ROWS)]
    finals = sum(
        closings[k][:4].astype(F32) + flags[k] * carried[k] for k in range(ROWS)
    ).astype(BF16)

    other = swapped(finals, 4 * ROWS)
    finals = finals + other
    other = swapped(finals, 2 * ROWS)
    width = out_weight.shape[1] // COLS
    out_weight = pltpu.with_memory_space_constraint(out_weight, pltpu.HBM)
    there = place[None].astype(jnp.int32)
    hidden, outgoing = pl.pallas_call(
        send_kernel,
        out_shape=(
            jax.ShapeDtypeStruct((local_rows, 4 * DV), BF16),
            jax.ShapeDtypeStruct((4, local_rows, width), BF16),
        ),
        in_specs=[SMEM] + [VMEM] * 5,
        out_specs=(VMEM,) * 2,
        name="send",
        compiler_params=pltpu.CompilerParams(vmem_limit_bytes=16 << 20),
    )(there, out, links, arriving, norm_gain[None, :], out_weight)
    incoming = lax.ppermute(outgoing, "head", [(i, i ^ 1) for i in range(COLS)])
    kept = pl.pallas_call(
        keep_kernel,
        out_shape=jax.ShapeDtypeStruct((4, local_rows, width), BF16),
        in_specs=[SMEM] + [VMEM] * 2,
        out_specs=VMEM,
        name="keep",
        compiler_params=pltpu.CompilerParams(vmem_limit_bytes=16 << 20),
    )(there, hidden, out_weight)
    sums = [kept[k].astype(F32) + incoming[k].astype(F32) for k in range(4)]
    parts = [sums[k].astype(BF16) for k in range(4)]
    finals, _ = lax.optimization_barrier((finals, parts[2]))
    finals = finals + other
    other = swapped(finals, ROWS)
    owners = row * ROWS + jnp.arange(ROWS, dtype=jnp.int32)
    chosen = (decode_owner[None, :] == owners[:, None])[:, :, None, None]
    finals = finals.astype(F32) + other.astype(F32)
    parcels = jnp.sum(jnp.where(chosen, finals[None], 0.0), axis=1).astype(BF16)
    owned = traded(parcels).astype(F32)

    moved = []
    for k in (2, 1, 3):
        moved.append(
            lax.ppermute(
                parts[k], "head", [(i, (i + 2 * k) % COLS) for i in range(COLS)]
            )
        )
    mixed = sums[0]
    for part in moved:
        mixed = mixed + part.astype(F32)
    mixed = mixed.astype(BF16)
    return (mixed, owned[None])


def solution(mesh):
    return jax.shard_map(
        program,
        mesh=mesh,
        in_specs=(
            P("seq", "head"),
            P("seq", "head"),
            P("seq", "head"),
            P("head", "seq"),
            P("head", "seq"),
            P(),
            P(),
            P(),
            P("head", None),
        ),
        out_specs=(P("seq", "head"), P("seq", "head", None, None)),
        check_vma=False,
    )
```
